512 devices in a mesh: cam: 16 (over x_lo, y), space: 32 (over x_hi, z, core).
Axes of the slice: x: 4 (x_hi: 2, x_lo: 2; x = x_hi * 2 + x_lo), y: 8, z: 8, core: 2. Of those that a mesh axis runs over, the one named last changes fastest.
Arguments:
- features: float32 [64, 131072], P(None, ('cam', 'space')), may hold values from -6 to 6
- positions: float32 [3, 131072], P(None, ('cam', 'space')), may hold values from -6144 to 6144, as said below
- spreads: float32 [131072], P(('cam', 'space')), may hold values from 16 to 64
- logits: float32 [131072], P(('cam', 'space')), may hold values from -6 to -2
- camera: float32 [16, 3], replicated, may hold values from -1 to 1
- decoder: bfloat16 [64, 512], replicated, may hold values from -0.75 to 0.75
- tile_lists: int32 [16, 32, 16, 256], P('cam', 'space'), may hold values from 0 to 8191, as said below
- counts: int32 [16, 32, 16], P('cam', 'space'), may hold values from 1 to 256, as said below
- targets: bfloat16 [16, 32, 16, 256, 512], P('cam', 'space'), may hold values from -6 to 6
Outputs:
- grad_features: float32 [64, 131072], P(None, ('cam', 'space'))
- grad_logits: float32 [131072], P(('cam', 'space'))
The draws below stay inside these ranges and needn't reach their ends.
Inputs may be any that keep to these rules, and one draw needn't show every extreme that they name: `positions`: rows are x, y and depth; depth lies between 4 and 8. `tile_lists`: the list of tile (c, s, j) names only ids j * 256 + q or 4096 + j * 256 + q with 0 <= q < 256, no id twice; lists of tile row 0 name only ids below 4096. `counts`: some tile has all 256 entries live.
All inputs are finite; a program needn't handle non-finite values.
Results may differ from the reference program's by a relative error of at most 0.003.
Values may be sent and summed in bfloat16 or wider, within the bound.
No kernel may reach another device: no remote copies, remote signals or barrier semaphores. Data moves between devices by JAX's collectives and lax.ppermute only.
A program may use at most 64 MiB of HBM per device.

```python
import math
import jax
import jax.numpy as jnp
from jax import lax

CH = 64
DEC = 512
TS = 16
L = 256
PIX = 256
VIEWS = 16
BANDS = 32
GAUSS = 131072


def draw_positions(key, part):
    count_all = L * VIEWS * BANDS
    row_index = jnp.arange(count_all)
    column = (row_index // (BANDS * L)).astype(jnp.float32)
    tile_row = (row_index // L % BANDS).astype(jnp.float32)
    key_across, key_down, key_depth = jax.random.split(key, 3)
    image_width = TS * VIEWS
    image_height = TS * BANDS
    offset_across = jax.random.uniform(key_across, (count_all,), jnp.float32, -0.5 * TS, 0.5 * TS)
    offset_down = jax.random.uniform(key_down, (count_all,), jnp.float32, -0.5 * TS, 1.5 * TS)
    distance = jax.random.uniform(key_depth, (count_all,), jnp.float32, 4.0, 8.0)
    centre_u = column * TS + 0.5 * TS - 0.5 * image_width + offset_across
    centre_v = tile_row * TS + 0.5 * TS - 0.5 * image_height + offset_down
    return jnp.stack([centre_u * distance, centre_v * distance, distance])


def draw_tile_lists(key, part):
    shape_tiles = (VIEWS, BANDS, VIEWS)
    key_first, key_second = jax.random.split(key)
    scores_two = jax.random.randint(key_first, shape_tiles + (2 * L,), 0, 2 ** 18) * (2 * L) + jnp.arange(2 * L)
    picked_two = jnp.argsort(scores_two, axis=-1, stable=True)[..., :L]
    scores_one = jax.random.randint(key_second, shape_tiles + (L,), 0, 2 ** 18) * L + jnp.arange(L)
    picked_one = jnp.argsort(scores_one, axis=-1, stable=True)
    tile_row = jnp.arange(BANDS)[None, :, None, None]
    column = jnp.arange(VIEWS)[None, None, :, None]
    chosen = jnp.where(tile_row == 0, picked_one, picked_two)
    block_rows = VIEWS * L
    return jnp.where(chosen < L, column * L + chosen, block_rows + column * L + chosen - L).astype(jnp.int32)


def draw_counts(key, part):
    key_density, key_count, key_peak = jax.random.split(key, 3)
    density = jax.random.randint(key_density, (VIEWS, BANDS, 1), 2, 5)
    ceiling = density * (L // 4)
    drawn = jax.random.randint(key_count, (VIEWS, BANDS, VIEWS), 0, ceiling) + 1
    peak = jax.random.randint(key_peak, (), 0, VIEWS * BANDS * VIEWS)
    flat_index = jnp.arange(VIEWS * BANDS * VIEWS).reshape(VIEWS, BANDS, VIEWS)
    return jnp.where(flat_index == peak, L, drawn).astype(jnp.int32)


def steps_of(rng, shape, pieces, least, largest):
    factor_of = 1.0
    for dim, blocks in pieces:
        steps = jax.random.uniform(jax.random.fold_in(jax.random.fold_in(rng, 6), dim), (blocks,), jnp.float32, least / len(pieces), largest / len(pieces))
        factor_of = factor_of * jnp.repeat(jnp.exp(steps), shape[dim] // blocks).reshape((-1,) + (1,) * (len(shape) - 1 - dim))
    return factor_of


def bell_draw(stream_key, extent, width, limit, shards=(), kind=jnp.bfloat16):
    level = steps_of(stream_key, extent, shards, -0.22, 0.18) if shards else 1.0
    values = jax.random.normal(stream_key, extent, jnp.float32) * width * level
    return jnp.minimum(jnp.maximum(values, -limit), limit).astype(kind)


def setup_inputs(seed: int = 0) -> dict:
    key_of = jax.random.split(jax.random.key(seed), 10)
    return {
        "features": bell_draw(key_of[0], (CH, GAUSS), 1.0, 6.0, ((1, 512),), jnp.float32),
        "positions": draw_positions(jax.random.fold_in(key_of[9], 71), 0),
        "spreads": jnp.clip(jnp.exp(math.log(64.0) - 1.3862944 * jax.random.uniform(key_of[2], (GAUSS,), jnp.float32) ** steps_of(key_of[2], (GAUSS,), ((0, 512),), -0.2, 0.2)), 16.0, 64.0),
        "logits": jnp.clip(-6.0 + 4.0 * jax.random.uniform(key_of[3], (GAUSS,), jnp.float32) ** steps_of(key_of[3], (GAUSS,), ((0, 512),), -0.2, 0.2), -6.0, -2.0),
        "camera": jnp.clip(jax.random.uniform(key_of[4], (VIEWS, 3), jnp.float32, -1.0, 1.0), -1.0, 1.0),
        "decoder": bell_draw(key_of[5], (CH, DEC), CH ** -0.5, 0.75),
        "tile_lists": draw_tile_lists(jax.random.fold_in(key_of[9], 71), 0),
        "counts": draw_counts(jax.random.fold_in(key_of[9], 71), 0),
        "targets": bell_draw(key_of[8], (VIEWS, BANDS, VIEWS, PIX, DEC), 1.0, 6.0, ((0, 16), (1, 32))),
    }


def rounded(value):
    return lax.optimization_barrier(value.astype(jnp.bfloat16)).astype(jnp.float32)


def tile_terms(gathered, viewers, tile_row, columns, live_counts, pixel_targets, decoder, image_width, image_height):
    channels = gathered.shape[0] - 5
    length = gathered.shape[2]
    distance = gathered[channels + 2] - 0.05 * viewers[:, 2:3]
    centre_u = (gathered[channels] - 0.75 * TS * viewers[:, 0:1]) / distance + 0.5 * image_width
    centre_v = (gathered[channels + 1] - 0.75 * TS * viewers[:, 1:2]) / distance + 0.5 * image_height
    radius = gathered[channels + 3] / distance
    sigmoid_open = jax.nn.sigmoid(gathered[channels + 4])
    opacity = 0.99 * sigmoid_open
    sigmoid_slope = 0.99 * sigmoid_open * (1.0 - sigmoid_open)
    pixel_id = jnp.arange(TS * TS).astype(jnp.int32)
    pixel_u = (columns[:, None] * TS + pixel_id[None, :] % TS).astype(jnp.float32) + 0.5
    pixel_v = (tile_row * TS + pixel_id // TS).astype(jnp.float32) + 0.5
    alive_mask = (jnp.arange(length).astype(jnp.int32)[None, :] < live_counts[:, None]).astype(jnp.float32)
    delta_u = pixel_u[:, :, None] - centre_u[:, None, :]
    delta_v = pixel_v[None, :, None] - centre_v[:, None, :]
    spread = radius[:, None, :]
    falloff = jnp.exp(-(delta_u * delta_u + delta_v * delta_v) / (2.0 * spread * spread))
    opaque = (opacity * alive_mask)[:, None, :] * falloff
    log_keep = jnp.log(1.0 - opaque)
    keep_to = jnp.exp(jnp.cumsum(log_keep, axis=2) - log_keep)
    weight = opaque * keep_to
    weight_bf = rounded(weight)
    feature_bf = rounded(gathered[:channels])
    composite = rounded(jnp.einsum("tpk,ctk->tcp", weight_bf, feature_bf))
    decoder_wide = decoder.astype(jnp.float32)
    decoded = jnp.einsum("tcp,cd->tpd", composite, decoder_wide)
    residual = decoded - pixel_targets.astype(jnp.float32)
    pixel_grad = rounded(jnp.einsum("tpd,cd->tcp", residual, decoder_wide))
    contrib = jnp.einsum("tcp,ctk->tpk", pixel_grad, feature_bf)
    feature_grad = jnp.einsum("tpk,tcp->ctk", weight_bf, pixel_grad)
    weighted = weight * contrib
    behind = jnp.sum(weighted, axis=2, keepdims=True) - jnp.cumsum(weighted, axis=2)
    dopaque = keep_to * contrib - behind / (1.0 - opaque)
    logit_grad = (alive_mask * sigmoid_slope) * jnp.sum(dopaque * falloff, axis=1)
    return feature_grad, logit_grad


def reference(features, positions, spreads, logits, camera, decoder, tile_lists, counts, targets):
    length = tile_lists.shape[-1]
    gauss_table = jnp.concatenate([features, positions, spreads[None], logits[None]], axis=0)
    block_rows = VIEWS * length
    image_width = TS * VIEWS
    image_height = TS * BANDS
    columns = jnp.arange(VIEWS).astype(jnp.int32)

    def visit_tile(totals, flat_index):
        camera_index = flat_index // BANDS
        tile_row = flat_index % BANDS
        entries = tile_lists[camera_index, tile_row]
        from_above = entries >= block_rows
        in_block = jnp.where(from_above, entries - block_rows, entries)
        source_row = jnp.where(from_above, tile_row - 1, tile_row)
        global_rows = ((in_block // length) * BANDS + source_row) * length + in_block % length
        gathered = jnp.take(gauss_table, global_rows, axis=1)
        viewers = jnp.broadcast_to(camera[camera_index], (VIEWS, 3))
        feature_grad, logit_grad = tile_terms(gathered, viewers, tile_row, columns, counts[camera_index, tile_row], targets[camera_index, tile_row], decoder, image_width, image_height)
        values = jnp.concatenate([feature_grad, logit_grad[None]], axis=0)
        return totals.at[:, global_rows].add(values), None

    zero_grads = jnp.zeros((features.shape[0] + 1, features.shape[1]), jnp.float32)
    totals, unused = lax.scan(visit_tile, zero_grads, jnp.arange(VIEWS * BANDS).astype(jnp.int32))
    return totals[:-1], totals[-1]
```

```python
import jax
import jax.numpy as jnp
from jax import lax
from jax.experimental import pallas as pl
from jax.experimental.pallas import tpu as pltpu
from jax.sharding import PartitionSpec as P

TS = 16
F32 = jnp.float32
BF16 = jnp.bfloat16
DEAD = 512.0
NN = (((1,), (0,)), ((), ()))
NT = (((1,), (1,)), ((), ()))
LOG2E = 1.4426950408889634


def dot(left, right, dims):
    return lax.dot_general(left, right, dims, preferred_element_type=F32)


def rolled(shard, axis, by):
    length = lax.axis_size(axis)
    return lax.ppermute(shard, axis, [(i, (i + by) % length) for i in range(length)])


def pieces(value):
    first = value.astype(BF16).astype(F32)
    rest = value - first
    second = rest.astype(BF16).astype(F32)
    third = (rest - second).astype(BF16).astype(F32)
    return first, second, third


def pack_kernel(ids_ref, counts_ref, decoder_ref, targets_ref, out_ref, codes_ref):
    tile = pl.program_id(0)
    tiles, length = ids_ref.shape
    segment = length // 8

    @pl.when(tile == 0)
    def _():
        ids = ids_ref[...]
        row = lax.broadcasted_iota(jnp.int32, (tiles, length), 0)
        entry = lax.broadcasted_iota(jnp.int32, (tiles, length), 1)
        above = ids >= tiles * length
        inside = jnp.where(above, ids - tiles * length, ids) - row * length
        code = jnp.where(above, -1 - inside, inside).astype(F32)
        code = jnp.where(entry < counts_ref[...], code, DEAD)
        source = lax.broadcasted_iota(jnp.int32, (length, length), 0)
        place = lax.broadcasted_iota(jnp.int32, (length, length), 1)
        chosen = source == segment * (place % 8) + place // 8
        codes_ref[...] = dot(code.astype(BF16), chosen.astype(F32).astype(BF16), NN)

    out_ref[0, 0:64, :] = dot(decoder_ref[...], targets_ref[0], NT)
    out_ref[0, 64:72, :] = jnp.broadcast_to(codes_ref[pl.ds(tile, 1), :], (8, length))


def prep_kernel(camera_ref, place_ref, own_ref, upper_ref, feature_ref, terms_ref, row_ref):
    channels, length = feature_ref.shape[0], own_ref.shape[1]
    feature_ref[:, 0:length] = own_ref[0:channels, :].astype(BF16)
    feature_ref[:, length:] = upper_ref[0:channels, :].astype(BF16)

    def both(row):
        return jnp.concatenate(
            [own_ref[row : row + 1, :], upper_ref[row : row + 1, :]], axis=1
        )

    place_x, place_y, depth, spread, logit = (both(channels + i) for i in range(5))
    log_open = LOG2E * (
        jnp.log(0.99) - (jnp.maximum(-logit, 0.0) + jnp.log(1.0 + jnp.exp(-jnp.abs(logit))))
    )
    row_ref[...] = jnp.zeros(row_ref.shape, F32)
    centre_u, centre_v = place_ref[0], place_ref[1]
    for view in range(terms_ref.shape[0]):
        distance = depth - 0.05 * camera_ref[view, 2]
        u = (place_x - 0.75 * TS * camera_ref[view, 0]) / distance + centre_u
        v = (place_y - 0.75 * TS * camera_ref[view, 1]) / distance + centre_v
        radius = spread / distance
        inverse = (0.5 * LOG2E) / (radius * radius)
        terms = (log_open - inverse * (u * u + v * v), 2.0 * inverse * u, 2.0 * inverse * v, -inverse)
        for index, term in enumerate(terms):
            for turn, piece in enumerate(pieces(term)):
                at = 3 * index + turn
                row_ref[at : at + 1, :] = piece
        terms_ref[view] = row_ref[...].astype(BF16)


def shift_rows(value, by, fill, index):
    moved = pltpu.roll(value, by % 8, 0)
    inside = index >= by if by > 0 else index < 8 + by
    return jnp.where(inside, moved, fill)


def tile_work(
    packed, terms, features, squares_ref, basis_ref, own_ref, upper_ref, a_ref, w_ref, wb_ref, ct_ref, ts_ref
):
    channels = features.shape[0]
    length = packed.shape[1]
    steps = length // 8
    code = packed[channels : channels + 1, :]
    slot = lax.broadcasted_iota(jnp.int32, (2 * length, length), 0)
    wanted = jnp.where(slot < length, slot, length - 1 - slot).astype(F32)
    hot = jnp.where(wanted == code, 1.0, 0.0).astype(BF16)
    picked = dot(jnp.concatenate([features, terms], axis=0), hot, NN)
    feature_t = picked[0:channels].astype(BF16)
    line = lax.broadcasted_iota(jnp.int32, picked.shape, 0)
    dead = jnp.where(code == DEAD, -32768.0, 0.0)
    entry_rows = jnp.where(line == channels + 12, dead, picked).T.astype(BF16)
    a_ref[...] = jnp.exp2(dot(entry_rows, basis_ref[...], NN))

    index = lax.broadcasted_iota(jnp.int32, (8, length), 0)
    keep = jnp.ones((8, length), F32)
    for i in range(steps):
        rows = pl.ds(8 * i, 8)
        local = a_ref[rows, :] * keep
        w_ref[rows, :] = local
        keep = keep - local
    start = shift_rows(keep, 1, 1.0, index)
    for by in (1, 2, 4):
        start = start * shift_rows(start, by, 1.0, index)
    for i in range(steps // 2):
        rows = pl.ds(16 * i, 16)
        wb_ref[rows, :] = (w_ref[rows, :] * jnp.concatenate([start, start], axis=0)).astype(BF16)
    weight_bf = wb_ref[...]
    composite = dot(feature_t, weight_bf, NN).astype(BF16)
    pixel_grad = (
        dot(squares_ref[...], jnp.concatenate([composite] * 3, axis=0), NN) - packed[0:channels, :]
    ).astype(BF16)
    padded = jnp.concatenate([pixel_grad, jnp.zeros((16, length), BF16)], axis=0)
    ct_ref[...] = dot(entry_rows, padded, NN)

    total = jnp.zeros((8, length), F32)
    for i in range(steps):
        rows = pl.ds(8 * i, 8)
        total = total + w_ref[rows, :] * ct_ref[rows, :]
    scale = keep
    for by in (1, 2, 4):
        total = total + scale * shift_rows(total, -by, 0.0, index)
        scale = scale * shift_rows(scale, -by, 1.0, index)
    after = shift_rows(total, -1, 0.0, index)
    for i in reversed(range(steps)):
        rows = pl.ds(8 * i, 8)
        gap = ct_ref[rows, :] - after
        term = (w_ref[rows, :] * start) * gap
        after = after + a_ref[rows, :] * gap
        ts_ref[rows, :] = term[:, 0:128] + term[:, 128:256]
    sums = ts_ref[...]
    sums_hi = sums.astype(BF16)
    sums_lo = (sums - sums_hi.astype(F32)).astype(BF16)
    ones = jnp.ones((8, length), BF16)
    logit_row = dot(ones, jnp.concatenate([sums_hi, sums_lo], axis=1), NT)
    feature_grad = dot(pixel_grad, weight_bf, NT)
    grad_hi = feature_grad.astype(BF16)
    grad_lo = (feature_grad - grad_hi.astype(F32)).astype(BF16)
    logit_hi = logit_row.astype(BF16).astype(F32)
    logit_both = jnp.concatenate([logit_hi, logit_row - logit_hi], axis=0).astype(BF16)
    values = jnp.concatenate([grad_hi, grad_lo, logit_both], axis=0)
    spread = dot(values, hot, NT)
    c = channels
    for ref, first in ((own_ref, 0), (upper_ref, length)):
        part = spread[:, first : first + length]
        ref[0:c, :] += part[0:c] + part[c : 2 * c]
        ref[c : c + 8, :] += part[2 * c : 2 * c + 8] + part[2 * c + 8 : 2 * c + 16]


def main_kernel(
    packed_ref, terms_ref, feature_ref, decoder_ref, own_ref, upper_ref, squares_ref, basis_ref, *scratch
):
    channels, length = feature_ref.shape[0], packed_ref.shape[2]

    @pl.when(pl.program_id(0) == 0)
    def _():
        own_ref[...] = jnp.zeros(own_ref.shape, F32)
        upper_ref[...] = jnp.zeros(upper_ref.shape, F32)
        for turn, piece in enumerate(pieces(dot(decoder_ref[...], decoder_ref[...], NT))):
            squares_ref[:, channels * turn : channels * (turn + 1)] = piece.astype(BF16)
        line = lax.broadcasted_iota(jnp.int32, basis_ref.shape, 0) - channels
        pixel = lax.broadcasted_iota(jnp.int32, basis_ref.shape, 1)
        px = (pixel % TS).astype(F32) - (0.5 * TS - 0.5)
        py = (pixel // TS).astype(F32) - (0.5 * TS - 0.5)
        basis = jnp.where(line < 3, 1.0, jnp.where(line < 6, px, jnp.where(line < 9, py, px * px + py * py)))
        basis = jnp.where(line == 12, 1.0, basis)
        basis_ref[...] = jnp.where((line < 0) | (line > 12), 0.0, basis).astype(BF16)

    for turn in range(packed_ref.shape[0]):
        tile_work(
            packed_ref[turn],
            terms_ref[turn],
            feature_ref[...],
            squares_ref,
            basis_ref,
            own_ref,
            upper_ref,
            *(ref.at[turn] for ref in scratch),
        )


def on_device(features, positions, spreads, logits, camera, decoder, tile_lists, counts, targets):
    channels, length = features.shape
    tiles = tile_lists.shape[2]
    decoded = decoder.shape[1]
    views = camera.shape[0]
    group = 2
    column = lax.axis_index("cam")
    tile_row = lax.axis_index("space")
    image_width = TS * lax.axis_size("cam")
    image_height = TS * lax.axis_size("space")

    packed = pl.pallas_call(
        pack_kernel,
        out_shape=jax.ShapeDtypeStruct((tiles, channels + 8, length), F32),
        grid=(tiles,),
        in_specs=[
            pl.BlockSpec((tiles, length), lambda t: (0, 0)),
            pl.BlockSpec((tiles, 1), lambda t: (0, 0)),
            pl.BlockSpec((channels, decoded), lambda t: (0, 0)),
            pl.BlockSpec((1, length, decoded), lambda t: (t, 0, 0)),
        ],
        out_specs=pl.BlockSpec((1, channels + 8, length), lambda t: (t, 0, 0)),
        scratch_shapes=[pltpu.VMEM((tiles, length), F32)],
        cost_estimate=pl.CostEstimate(
            flops=2 * tiles * length * channels * decoded,
            bytes_accessed=tiles * length * (2 * decoded + 4 * channels),
            transcendentals=0,
        ),
        name="pack",
    )(tile_lists[0, 0], counts[0, 0][:, None], decoder, targets[0, 0])
    received = lax.all_to_all(packed, "cam", 0, 0, tiled=True)

    own_slab = jnp.concatenate([features, positions, spreads[None], logits[None]], axis=0)
    upper_slab = rolled(own_slab, "space", 1)
    place = jnp.stack(
        [
            0.5 * image_width - (column * TS + 0.5 * TS),
            0.5 * image_height - (tile_row * TS + 0.5 * TS),
        ]
    ).astype(F32)
    feature_bf, terms = pl.pallas_call(
        prep_kernel,
        out_shape=(
            jax.ShapeDtypeStruct((channels, 2 * length), BF16),
            jax.ShapeDtypeStruct((views, 16, 2 * length), BF16),
        ),
        in_specs=[
            pl.BlockSpec(memory_space=pltpu.SMEM),
            pl.BlockSpec(memory_space=pltpu.SMEM),
            pl.BlockSpec(memory_space=pltpu.VMEM),
            pl.BlockSpec(memory_space=pltpu.VMEM),
        ],
        out_specs=(
            pl.BlockSpec(memory_space=pltpu.VMEM),
            pl.BlockSpec(memory_space=pltpu.VMEM),
        ),
        scratch_shapes=[pltpu.VMEM((16, 2 * length), F32)],
        cost_estimate=pl.CostEstimate(flops=10000000, bytes_accessed=1000000, transcendentals=20000),
        name="prep",
    )(camera, place, own_slab, upper_slab)

    own_sum, upper_sum = pl.pallas_call(
        main_kernel,
        out_shape=(jax.ShapeDtypeStruct((channels + 8, length), F32),) * 2,
        grid=(views // group,),
        in_specs=[
            pl.BlockSpec((group, channels + 8, length), lambda t: (t, 0, 0)),
            pl.BlockSpec((group, 16, 2 * length), lambda t: (t, 0, 0)),
            pl.BlockSpec((channels, 2 * length), lambda t: (0, 0)),
            pl.BlockSpec((channels, decoded), lambda t: (0, 0)),
        ],
        out_specs=(pl.BlockSpec((channels + 8, length), lambda t: (0, 0)),) * 2,
        scratch_shapes=[
            pltpu.VMEM((channels, 3 * channels), BF16),
            pltpu.VMEM((channels + 16, length), BF16),
            pltpu.VMEM((group, length, length), F32),
            pltpu.VMEM((group, length, length), F32),
            pltpu.VMEM((group, length, length), BF16),
            pltpu.VMEM((group, length, length), F32),
            pltpu.VMEM((group, length, 128), F32),
        ],
        cost_estimate=pl.CostEstimate(
            flops=views * 2 * length * length * 1000, bytes_accessed=2000000, transcendentals=views * length * length
        ),
        name="splat",
    )(received, terms, feature_bf, decoder)
    returned = rolled(upper_sum, "space", -1)
    summed = own_sum + returned
    return summed[:channels], summed[channels] * (1.0 - jax.nn.sigmoid(logits))


def solution(mesh):
    placed = (
        P(None, ("cam", "space")),
        P(None, ("cam", "space")),
        P(("cam", "space")),
        P(("cam", "space")),
        P(),
        P(),
        P("cam", "space", None, None),
        P("cam", "space", None),
        P("cam", "space", None, None, None),
    )
    return jax.shard_map(
        on_device,
        mesh=mesh,
        in_specs=placed,
        out_specs=(P(None, ("cam", "space")), P(("cam", "space"))),
        check_vma=False,
    )
```

```python
import jax
import jax.numpy as jnp
from jax import lax
from jax.experimental import pallas as pl
from jax.experimental.pallas import tpu as pltpu
from jax.sharding import PartitionSpec as P

TS = 16
F32 = jnp.float32
BF16 = jnp.bfloat16
DEAD = 512.0
FULL = 32000.0
NN = (((1,), (0,)), ((), ()))
NT = (((1,), (1,)), ((), ()))
LOG2E = 1.4426950408889634


def dot(left, right, dims):
    return lax.dot_general(left, right, dims, preferred_element_type=F32)


def shifted(shard, axis, by):
    length = lax.axis_size(axis)
    pairs = [(i, i + by) for i in range(length) if 0 <= i + by < length]
    return lax.ppermute(shard, axis, pairs)


def pieces(value):
    first = value.astype(BF16).astype(F32)
    rest = value - first
    second = rest.astype(BF16).astype(F32)
    third = (rest - second).astype(BF16).astype(F32)
    return first, second, third


def list_kernel(ids_ref, counts_ref, out_ref):
    tiles, length = ids_ref.shape
    segment = length // 8
    ids = ids_ref[...]
    row = lax.broadcasted_iota(jnp.int32, (tiles, length), 0)
    entry = lax.broadcasted_iota(jnp.int32, (tiles, length), 1)
    above = ids >= tiles * length
    inside = jnp.where(above, ids - tiles * length, ids) - row * length
    code = jnp.where(above, -1 - inside, inside).astype(F32)
    live = jnp.zeros((tiles, length), jnp.int32)
    for tile in range(tiles):
        live = jnp.where(row == tile, counts_ref[tile], live)
    code = jnp.where(entry < live, code, DEAD)
    source = lax.broadcasted_iota(jnp.int32, (length, length), 0)
    place = lax.broadcasted_iota(jnp.int32, (length, length), 1)
    chosen = source == segment * (place % 8) + place // 8
    codes = dot(code.astype(BF16), chosen.astype(F32).astype(BF16), NN).astype(jnp.int32)
    for tile in range(tiles):
        out_ref[tile] = jnp.broadcast_to(codes[tile : tile + 1, :], (8, length)).astype(jnp.int16)


def pack_kernel(decoder_ref, targets_ref, out_ref):
    channels = decoder_ref.shape[0]
    for turn in range(targets_ref.shape[0]):
        value = dot(targets_ref[turn], decoder_ref[...], NT).T
        largest = jnp.max(jnp.abs(value), axis=0, keepdims=True)
        power = jnp.floor(jnp.log2(jnp.maximum(largest, 1e-30))) + 1.0
        fixed = jnp.round(value * (FULL * jnp.exp2(-power)))
        out_ref[turn, 0:channels, :] = fixed.astype(jnp.int32).astype(jnp.int16)
        powers = jnp.broadcast_to(power, (8, value.shape[1]))
        out_ref[turn, channels : channels + 8, :] = powers.astype(jnp.int32).astype(jnp.int16)


def prep_kernel(camera_ref, place_ref, own_ref, upper_ref, feature_ref, terms_ref, row_ref):
    channels, length = feature_ref.shape[0], own_ref.shape[1]
    feature_ref[:, 0:length] = own_ref[0:channels, :].astype(BF16)
    feature_ref[:, length:] = upper_ref[0:channels, :].astype(BF16)

    def both(row):
        own = own_ref[row : row + 1, :]
        return jnp.concatenate([own, jnp.where(place_ref[2] > 0.0, upper_ref[row : row + 1, :], own)], axis=1)

    place_x, place_y, depth, spread, logit = (both(channels + i) for i in range(5))
    log_open = LOG2E * (
        jnp.log(0.99) - (jnp.maximum(-logit, 0.0) + jnp.log(1.0 + jnp.exp(-jnp.abs(logit))))
    )
    row_ref[...] = jnp.zeros(row_ref.shape, F32)
    centre_u, centre_v = place_ref[0], place_ref[1]
    for view in range(terms_ref.shape[0]):
        distance = depth - 0.05 * camera_ref[view, 2]
        u = (place_x - 0.75 * TS * camera_ref[view, 0]) / distance + centre_u
        v = (place_y - 0.75 * TS * camera_ref[view, 1]) / distance + centre_v
        radius = spread / distance
        inverse = (0.5 * LOG2E) / (radius * radius)
        terms = (log_open - inverse * (u * u + v * v), 2.0 * inverse * u, 2.0 * inverse * v, -inverse)
        for index, term in enumerate(terms):
            for turn, piece in enumerate(pieces(term)):
                at = 3 * index + turn
                row_ref[at : at + 1, :] = piece
        terms_ref[view] = row_ref[...].astype(BF16)


def shift_rows(value, by, fill, index):
    moved = pltpu.roll(value, by % 8, 0)
    inside = index >= by if by > 0 else index < 8 + by
    return jnp.where(inside, moved, fill)


def in_turns(works):
    works = list(works)
    while works:
        works = [work for work in works if next(work, None) is not None]


def hot_rows(wanted_ref, codes, hot_ref):
    code = jnp.concatenate([codes, codes], axis=0).astype(BF16)
    half = wanted_ref.shape[1]
    one, zero = jnp.ones((16, half), BF16), jnp.zeros((16, half), BF16)
    for first in range(0, hot_ref.shape[0], 16):
        wanted = wanted_ref[first : first + 16, :]
        for side in range(0, code.shape[1], half):
            hot_ref[first : first + 16, side : side + half] = jnp.where(
                wanted == code[:, side : side + half], one, zero
            )


def set_wanted(wanted_ref):
    slot = lax.broadcasted_iota(jnp.int32, wanted_ref.shape, 0)
    length = wanted_ref.shape[0] // 2
    wanted_ref[...] = jnp.where(slot < length, slot, length - 1 - slot).astype(F32).astype(BF16)


def forward_tile(
    codes_ref, terms_ref, feature_ref, squares_ref, basis_ref, wanted_ref,
    entry_ref, a_ref, w_ref, wb_ref, ends_ref, projected_ref, hot_ref
):
    channels = feature_ref.shape[0]
    length = codes_ref.shape[1]
    steps = length // 8
    codes = codes_ref[...].astype(jnp.int32).astype(F32)
    hot_rows(wanted_ref, codes, hot_ref)
    yield True
    table = jnp.concatenate([feature_ref[...], terms_ref[...]], axis=0)
    picked = dot(table, hot_ref[...], NN)
    feature_t = picked[0:channels].astype(BF16)
    line = lax.broadcasted_iota(jnp.int32, (16, length), 0)
    dead = jnp.where(codes[0:1, :] == DEAD, -32768.0, 0.0)
    lower = jnp.where(line == 12, dead, picked[channels:])
    entry_ref[...] = jnp.concatenate([picked[0:channels], lower], axis=0).T.astype(BF16)
    yield True
    for first in range(0, length, 64):
        a_ref[first : first + 64, :] = jnp.exp2(dot(entry_ref[first : first + 64, :], basis_ref[...], NN))
    yield True
    index = lax.broadcasted_iota(jnp.int32, (8, length), 0)
    keep = jnp.ones((8, length), F32)
    for i in range(steps):
        rows = pl.ds(8 * i, 8)
        local = a_ref[rows, :] * keep
        w_ref[rows, :] = local
        keep = keep - local
    start = shift_rows(keep, 1, 1.0, index)
    for by in (1, 2, 4):
        start = start * shift_rows(start, by, 1.0, index)
    ends_ref[0:8, :] = start
    ends_ref[8:16, :] = keep
    yield True
    for i in range(steps // 2):
        rows = pl.ds(16 * i, 16)
        wb_ref[rows, :] = (w_ref[rows, :] * jnp.concatenate([start, start], axis=0)).astype(BF16)
    yield True
    composite = dot(feature_t, wb_ref[...], NN).astype(BF16)
    projected_ref[...] = dot(squares_ref[...], jnp.concatenate([composite] * 3, axis=0), NN)


def forward_kernel(
    codes_ref, terms_ref, feature_ref, decoder_ref,
    entry_ref, a_ref, w_ref, wb_ref, ends_ref, projected_ref,
    squares_ref, basis_ref, wanted_ref, hot_ref
):
    channels = feature_ref.shape[0]

    @pl.when(pl.program_id(0) == 0)
    def _():
        set_wanted(wanted_ref)
        for turn, piece in enumerate(pieces(dot(decoder_ref[...], decoder_ref[...], NT))):
            squares_ref[:, channels * turn : channels * (turn + 1)] = piece.astype(BF16)
        line = lax.broadcasted_iota(jnp.int32, basis_ref.shape, 0) - channels
        pixel = lax.broadcasted_iota(jnp.int32, basis_ref.shape, 1)
        px = (pixel % TS).astype(F32) - (0.5 * TS - 0.5)
        py = (pixel // TS).astype(F32) - (0.5 * TS - 0.5)
        basis = jnp.where(line < 3, 1.0, jnp.where(line < 6, px, jnp.where(line < 9, py, px * px + py * py)))
        basis = jnp.where(line == 12, 1.0, basis)
        basis_ref[...] = jnp.where((line < 0) | (line > 12), 0.0, basis).astype(BF16)

    in_turns(
        forward_tile(
            codes_ref.at[turn], terms_ref.at[turn],
            feature_ref, squares_ref, basis_ref, wanted_ref,
            *(ref.at[turn] for ref in (entry_ref, a_ref, w_ref, wb_ref, ends_ref, projected_ref, hot_ref)),
        )
        for turn in range(hot_ref.shape[0])
    )


def backward_tile(
    packed_ref, codes_ref, entry_ref, a_ref, w_ref, wb_ref, ends_ref, projected_ref, wanted_ref,
    own_ref, upper_ref, hot_ref, ct_ref, ts_ref
):
    channels, length = projected_ref.shape
    steps = length // 8
    index = lax.broadcasted_iota(jnp.int32, (8, length), 0)
    packed = packed_ref[...].astype(jnp.int32).astype(F32)
    scale = jnp.exp2(packed[channels : channels + 1, :]) * (1.0 / FULL)
    pixel_grad = (projected_ref[...] - packed[0:channels] * scale).astype(BF16)
    padded = jnp.concatenate([pixel_grad, jnp.zeros((16, length), BF16)], axis=0)
    yield True
    total = jnp.zeros((8, length), F32)
    for first in range(0, length, 64):
        ct = dot(entry_ref[first : first + 64, :], padded, NN)
        ct_ref[first : first + 64, :] = ct
        for i in range(8):
            total = total + w_ref[pl.ds(first + 8 * i, 8), :] * ct[8 * i : 8 * i + 8, :]
    yield True
    start, factor = ends_ref[0:8, :], ends_ref[8:16, :]
    for by in (1, 2, 4):
        total = total + factor * shift_rows(total, -by, 0.0, index)
        factor = factor * shift_rows(factor, -by, 1.0, index)
    after = shift_rows(total, -1, 0.0, index)
    for i in reversed(range(steps)):
        rows = pl.ds(8 * i, 8)
        gap = ct_ref[rows, :] - after
        term = (w_ref[rows, :] * start) * gap
        after = after + a_ref[rows, :] * gap
        ts_ref[rows, :] = term[:, 0:128] + term[:, 128:256]
    yield True
    feature_grad = dot(pixel_grad, wb_ref[...], NT)
    hot_rows(wanted_ref, codes_ref[...].astype(jnp.int32).astype(F32), hot_ref)
    yield True
    sums = ts_ref[...]
    sums_hi = sums.astype(BF16)
    sums_lo = (sums - sums_hi.astype(F32)).astype(BF16)
    ones = jnp.ones((8, length), BF16)
    logit_row = dot(ones, jnp.concatenate([sums_hi, sums_lo], axis=1), NT)
    grad_hi = feature_grad.astype(BF16)
    grad_lo = (feature_grad - grad_hi.astype(F32)).astype(BF16)
    logit_hi = logit_row.astype(BF16).astype(F32)
    logit_both = jnp.concatenate([logit_hi, logit_row - logit_hi], axis=0).astype(BF16)
    values = jnp.concatenate([grad_hi, grad_lo, logit_both], axis=0)
    yield True
    spread = dot(values, hot_ref[...], NT)
    c = channels
    for ref, first in ((own_ref, 0), (upper_ref, length)):
        part = spread[:, first : first + length]
        ref[0:c, :] += part[0:c] + part[c : 2 * c]
        ref[c : c + 8, :] += part[2 * c : 2 * c + 8] + part[2 * c + 8 : 2 * c + 16]


def backward_kernel(
    packed_ref, codes_ref, entry_ref, a_ref, w_ref, wb_ref, ends_ref, projected_ref,
    own_ref, upper_ref, wanted_ref, hot_ref, ct_ref, ts_ref
):
    @pl.when(pl.program_id(0) == 0)
    def _():
        set_wanted(wanted_ref)
        own_ref[...] = jnp.zeros(own_ref.shape, F32)
        upper_ref[...] = jnp.zeros(upper_ref.shape, F32)

    in_turns(
        backward_tile(
            *(
                ref.at[turn]
                for ref in (packed_ref, codes_ref, entry_ref, a_ref, w_ref, wb_ref, ends_ref, projected_ref)
            ),
            wanted_ref, own_ref, upper_ref, hot_ref.at[turn], ct_ref.at[turn], ts_ref.at[turn],
        )
        for turn in range(hot_ref.shape[0])
    )


def finish_kernel(own_ref, returned_ref, logits_ref, feature_ref, logit_ref):
    channels = feature_ref.shape[0]
    feature_ref[...] = own_ref[0:channels, :] + returned_ref[0:channels, :]
    summed = own_ref[channels : channels + 1, :] + returned_ref[channels : channels + 1, :]
    logit_ref[...] = summed / (1.0 + jnp.exp(logits_ref[...]))


def whole():
    return pl.BlockSpec(memory_space=pltpu.VMEM)


def small():
    return pltpu.CompilerParams(vmem_limit_bytes=8 << 20)


def blocks(group, *shape):
    return pl.BlockSpec((group,) + shape, lambda t: (t,) + (0,) * len(shape))


def fixed(*shape):
    return pl.BlockSpec(shape, lambda t: (0,) * len(shape))


def on_device(features, positions, spreads, logits, camera, decoder, tile_lists, counts, targets):
    channels, length = features.shape
    tiles = tile_lists.shape[2]
    decoded = decoder.shape[1]
    views = camera.shape[0]
    pack_group, group = 2, 2
    column = lax.axis_index("cam")
    tile_row = lax.axis_index("space")
    image_width = TS * lax.axis_size("cam")
    image_height = TS * lax.axis_size("space")
    shape = jax.ShapeDtypeStruct

    coded = pl.pallas_call(
        list_kernel,
        out_shape=shape((tiles, 8, length), jnp.int16),
        in_specs=[whole(), pl.BlockSpec(memory_space=pltpu.SMEM)],
        out_specs=whole(),
        compiler_params=small(),
        cost_estimate=pl.CostEstimate(flops=1000000, bytes_accessed=100000, transcendentals=0),
        name="lists",
    )(tile_lists[0, 0], counts[0, 0])
    codes = lax.all_to_all(coded, "cam", 0, 0, tiled=True)
    own_slab = jnp.concatenate([features, positions, spreads[None], logits[None]], axis=0)
    upper_slab = shifted(own_slab, "space", 1)

    packed = pl.pallas_call(
        pack_kernel,
        out_shape=shape((tiles, channels + 8, length), jnp.int16),
        grid=(tiles // pack_group,),
        in_specs=[fixed(channels, decoded), blocks(pack_group, length, decoded)],
        out_specs=blocks(pack_group, channels + 8, length),
        cost_estimate=pl.CostEstimate(
            flops=2 * tiles * length * channels * decoded,
            bytes_accessed=tiles * length * (2 * decoded + 2 * channels),
            transcendentals=0,
        ),
        name="pack",
    )(decoder, targets[0, 0])
    packed, upper_slab = lax.optimization_barrier((packed, upper_slab))
    received = lax.all_to_all(packed, "cam", 0, 0, tiled=True)

    place = jnp.stack(
        [
            0.5 * image_width - (column * TS + 0.5 * TS),
            0.5 * image_height - (tile_row * TS + 0.5 * TS),
            tile_row,
        ]
    ).astype(F32)
    feature_bf, terms = pl.pallas_call(
        prep_kernel,
        out_shape=(shape((channels, 2 * length), BF16), shape((views, 16, 2 * length), BF16)),
        in_specs=[
            pl.BlockSpec(memory_space=pltpu.SMEM),
            pl.BlockSpec(memory_space=pltpu.SMEM),
            whole(),
            whole(),
        ],
        out_specs=(whole(), whole()),
        scratch_shapes=[pltpu.VMEM((16, 2 * length), F32)],
        cost_estimate=pl.CostEstimate(flops=10000000, bytes_accessed=1000000, transcendentals=20000),
        name="prep",
    )(camera, place, own_slab, upper_slab)

    kept = (
        ((length, channels + 16), BF16),
        ((length, length), F32),
        ((length, length), F32),
        ((length, length), BF16),
        ((16, length), F32),
        ((channels, length), F32),
    )
    saved = pl.pallas_call(
        forward_kernel,
        out_shape=tuple(shape((views,) + size, kind) for size, kind in kept),
        grid=(views // group,),
        in_specs=[
            blocks(group, 8, length),
            blocks(group, 16, 2 * length),
            fixed(channels, 2 * length),
            fixed(channels, decoded),
        ],
        out_specs=tuple(blocks(group, *size) for size, _ in kept),
        scratch_shapes=[
            pltpu.VMEM((channels, 3 * channels), BF16),
            pltpu.VMEM((channels + 16, length), BF16),
            pltpu.VMEM((2 * length, 128), BF16),
            pltpu.VMEM((group, 2 * length, length), BF16),
        ],
        cost_estimate=pl.CostEstimate(
            flops=views * 2 * length * length * 600,
            bytes_accessed=views * length * length * 11,
            transcendentals=views * length * length,
        ),
        name="forward",
    )(codes, terms, feature_bf, decoder)

    own_sum, upper_sum = pl.pallas_call(
        backward_kernel,
        out_shape=(shape((channels + 8, length), F32),) * 2,
        grid=(views // group,),
        in_specs=[
            blocks(group, channels + 8, length),
            blocks(group, 8, length),
            *(blocks(group, *size) for size, _ in kept),
        ],
        out_specs=(whole(),) * 2,
        scratch_shapes=[
            pltpu.VMEM((2 * length, 128), BF16),
            pltpu.VMEM((group, 2 * length, length), BF16),
            pltpu.VMEM((group, length, length), F32),
            pltpu.VMEM((group, length, 128), F32),
        ],
        cost_estimate=pl.CostEstimate(
            flops=views * 2 * length * length * 600,
            bytes_accessed=views * length * length * 11,
            transcendentals=0,
        ),
        name="backward",
    )(received, codes, *saved)
    returned = shifted(upper_sum, "space", -1)
    grad_features, grad_logits = pl.pallas_call(
        finish_kernel,
        out_shape=(shape((channels, length), F32), shape((1, length), F32)),
        in_specs=[whole(), whole(), whole()],
        out_specs=(whole(), whole()),
        compiler_params=small(),
        name="finish",
    )(own_sum, returned, logits[None])
    return grad_features, grad_logits[0]


def solution(mesh):
    placed = (
        P(None, ("cam", "space")),
        P(None, ("cam", "space")),
        P(("cam", "space")),
        P(("cam", "space")),
        P(),
        P(),
        P("cam", "space", None, None),
        P("cam", "space", None),
        P("cam", "space", None, None, None),
    )
    return jax.shard_map(
        on_device,
        mesh=mesh,
        in_specs=placed,
        out_specs=(P(None, ("cam", "space")), P(("cam", "space"))),
        check_vma=False,
    )
```

```python
import jax
import jax.numpy as jnp
from jax import lax
from jax.experimental import pallas as pl
from jax.experimental.pallas import tpu as pltpu
from jax.sharding import PartitionSpec as P

TS = 16
F32 = jnp.float32
BF16 = jnp.bfloat16
DEAD = 512.0
FULL = 32000.0
NN = (((1,), (0,)), ((), ()))
NT = (((1,), (1,)), ((), ()))
LOG2E = 1.4426950408889634


def dot(left, right, dims):
    return lax.dot_general(left, right, dims, preferred_element_type=F32)


def shifted(shard, axis, by):
    length = lax.axis_size(axis)
    pairs = [(i, i + by) for i in range(length) if 0 <= i + by < length]
    return lax.ppermute(shard, axis, pairs)


def pieces(value):
    first = value.astype(BF16).astype(F32)
    rest = value - first
    second = rest.astype(BF16).astype(F32)
    third = (rest - second).astype(BF16).astype(F32)
    return first, second, third


def list_kernel(ids_ref, counts_ref, out_ref):
    tiles, length = ids_ref.shape
    segment = length // 8
    ids = ids_ref[...]
    row = lax.broadcasted_iota(jnp.int32, (tiles, length), 0)
    entry = lax.broadcasted_iota(jnp.int32, (tiles, length), 1)
    above = ids >= tiles * length
    inside = jnp.where(above, ids - tiles * length, ids) - row * length
    code = jnp.where(above, -1 - inside, inside).astype(F32)
    live = jnp.zeros((tiles, length), jnp.int32)
    for tile in range(tiles):
        live = jnp.where(row == tile, counts_ref[tile], live)
    code = jnp.where(entry < live, code, DEAD)
    source = lax.broadcasted_iota(jnp.int32, (length, length), 0)
    place = lax.broadcasted_iota(jnp.int32, (length, length), 1)
    chosen = source == segment * (place % 8) + place // 8
    codes = dot(code.astype(BF16), chosen.astype(F32).astype(BF16), NN).astype(jnp.int32)
    for tile in range(tiles):
        out_ref[tile] = jnp.broadcast_to(codes[tile : tile + 1, :], (8, length)).astype(jnp.int16)


def pack_kernel(decoder_ref, targets_ref, out_ref, held_ref, built_ref, in_sem, out_sem):
    channels = decoder_ref.shape[0]
    tiles = held_ref.shape[0]
    group = tiles // out_sem.shape[0]

    def incoming(tile):
        return pltpu.make_async_copy(targets_ref.at[tile], held_ref.at[tile], in_sem.at[tile])

    def outgoing(turn):
        span = pl.ds(turn * group, group)
        return pltpu.make_async_copy(built_ref.at[span], out_ref.at[span], out_sem.at[turn])

    for tile in range(tiles):
        incoming(tile).start()

    def build(turn, carry):
        for step in range(group):
            incoming(turn * group + step).wait()
        for step in range(group):
            tile = turn * group + step
            value = dot(held_ref[tile], decoder_ref[...], NT).T
            largest = jnp.max(jnp.abs(value), axis=0, keepdims=True)
            power = jnp.floor(jnp.log2(jnp.maximum(largest, 1e-30))) + 1.0
            fixed_point = jnp.round(value * (FULL * jnp.exp2(-power)))
            built_ref[tile, 0:channels, :] = fixed_point.astype(jnp.int32).astype(jnp.int16)
            powers = jnp.broadcast_to(power, (8, value.shape[1]))
            built_ref[tile, channels : channels + 8, :] = powers.astype(jnp.int32).astype(jnp.int16)
        outgoing(turn).start()
        return carry

    lax.fori_loop(0, out_sem.shape[0], build, 0)
    for turn in range(out_sem.shape[0]):
        outgoing(turn).wait()


def prep_kernel(camera_ref, place_ref, own_ref, upper_ref, feature_ref, terms_ref, row_ref):
    channels, length = feature_ref.shape[0], own_ref.shape[1]
    feature_ref[:, 0:length] = own_ref[0:channels, :].astype(BF16)
    feature_ref[:, length:] = upper_ref[0:channels, :].astype(BF16)

    def both(row):
        own = own_ref[row : row + 1, :]
        return jnp.concatenate([own, jnp.where(place_ref[2] > 0.0, upper_ref[row : row + 1, :], own)], axis=1)

    place_x, place_y, depth, spread, logit = (both(channels + i) for i in range(5))
    log_open = LOG2E * (
        jnp.log(0.99) - (jnp.maximum(-logit, 0.0) + jnp.log(1.0 + jnp.exp(-jnp.abs(logit))))
    )
    row_ref[...] = jnp.zeros(row_ref.shape, F32)
    centre_u, centre_v = place_ref[0], place_ref[1]
    for view in range(terms_ref.shape[0]):
        distance = depth - 0.05 * camera_ref[view, 2]
        u = (place_x - 0.75 * TS * camera_ref[view, 0]) / distance + centre_u
        v = (place_y - 0.75 * TS * camera_ref[view, 1]) / distance + centre_v
        radius = spread / distance
        inverse = (0.5 * LOG2E) / (radius * radius)
        terms = (log_open - inverse * (u * u + v * v), 2.0 * inverse * u, 2.0 * inverse * v, -inverse)
        for index, term in enumerate(terms):
            for turn, piece in enumerate(pieces(term)):
                at = 3 * index + turn
                row_ref[at : at + 1, :] = piece
        terms_ref[view] = row_ref[...].astype(BF16)


def shift_rows(value, by, fill, index):
    moved = pltpu.roll(value, by % 8, 0)
    inside = index >= by if by > 0 else index < 8 + by
    return jnp.where(inside, moved, fill)


def in_turns(works, before=()):
    works, stage = list(works), 0
    while works:
        if stage < len(before):
            before[stage]()
        works = [work for work in works if next(work, None) is not None]
        stage += 1


def hot_rows(wanted_ref, codes, hot_ref):
    code = jnp.concatenate([codes, codes], axis=0).astype(BF16)
    half = wanted_ref.shape[1]
    one, zero = jnp.ones((16, half), BF16), jnp.zeros((16, half), BF16)
    for first in range(0, hot_ref.shape[0], 16):
        wanted = wanted_ref[first : first + 16, :]
        for side in range(0, code.shape[1], half):
            hot_ref[first : first + 16, side : side + half] = jnp.where(
                wanted == code[:, side : side + half], one, zero
            )


def set_wanted(wanted_ref):
    slot = lax.broadcasted_iota(jnp.int32, wanted_ref.shape, 0)
    length = wanted_ref.shape[0] // 2
    wanted_ref[...] = jnp.where(slot < length, slot, length - 1 - slot).astype(F32).astype(BF16)


def forward_tile(
    codes_ref, terms_ref, feature_ref, squares_ref, basis_ref, wanted_ref,
    entry_ref, a_ref, w_ref, wb_ref, ends_ref, projected_ref, hot_ref
):
    channels = feature_ref.shape[0]
    length = codes_ref.shape[1]
    steps = length // 8
    codes = codes_ref[...].astype(jnp.int32).astype(F32)
    hot_rows(wanted_ref, codes, hot_ref)
    yield True
    table = jnp.concatenate([feature_ref[...], terms_ref[...]], axis=0)
    picked = dot(table, hot_ref[...], NN)
    feature_t = picked[0:channels].astype(BF16)
    line = lax.broadcasted_iota(jnp.int32, (16, length), 0)
    dead = jnp.where(codes[0:1, :] == DEAD, -32768.0, 0.0)
    lower = jnp.where(line == 12, dead, picked[channels:])
    entry_ref[...] = jnp.concatenate([picked[0:channels], lower], axis=0).T.astype(BF16)
    yield True
    for first in range(0, length, 64):
        a_ref[first : first + 64, :] = jnp.exp2(dot(entry_ref[first : first + 64, :], basis_ref[...], NN))
    yield True
    index = lax.broadcasted_iota(jnp.int32, (8, length), 0)
    keep = jnp.ones((8, length), F32)
    for i in range(steps):
        rows = pl.ds(8 * i, 8)
        local = a_ref[rows, :] * keep
        w_ref[rows, :] = local
        keep = keep - local
    start = shift_rows(keep, 1, 1.0, index)
    for by in (1, 2, 4):
        start = start * shift_rows(start, by, 1.0, index)
    ends_ref[0:8, :] = start
    ends_ref[8:16, :] = keep
    yield True
    both = jnp.concatenate([start, start], axis=0)
    for i in range(steps // 2):
        rows = pl.ds(16 * i, 16)
        weight = w_ref[rows, :] * both
        w_ref[rows, :] = weight
        wb_ref[rows, :] = weight.astype(BF16)
    yield True
    composite = dot(feature_t, wb_ref[...], NN).astype(BF16)
    projected_ref[...] = dot(squares_ref[...], jnp.concatenate([composite] * 3, axis=0), NN)


def forward_kernel(
    codes_ref, terms_ref, feature_ref, decoder_ref,
    entry_ref, a_ref, w_ref, wb_ref, ends_ref, projected_ref,
    squares_ref, basis_ref, wanted_ref, hot_ref
):
    channels = feature_ref.shape[0]

    @pl.when(pl.program_id(0) == 0)
    def _():
        set_wanted(wanted_ref)
        for turn, piece in enumerate(pieces(dot(decoder_ref[...], decoder_ref[...], NT))):
            squares_ref[:, channels * turn : channels * (turn + 1)] = piece.astype(BF16)
        line = lax.broadcasted_iota(jnp.int32, basis_ref.shape, 0) - channels
        pixel = lax.broadcasted_iota(jnp.int32, basis_ref.shape, 1)
        px = (pixel % TS).astype(F32) - (0.5 * TS - 0.5)
        py = (pixel // TS).astype(F32) - (0.5 * TS - 0.5)
        basis = jnp.where(line < 3, 1.0, jnp.where(line < 6, px, jnp.where(line < 9, py, px * px + py * py)))
        basis = jnp.where(line == 12, 1.0, basis)
        basis_ref[...] = jnp.where((line < 0) | (line > 12), 0.0, basis).astype(BF16)

    in_turns(
        forward_tile(
            codes_ref.at[turn], terms_ref.at[turn],
            feature_ref, squares_ref, basis_ref, wanted_ref,
            *(ref.at[turn] for ref in (entry_ref, a_ref, w_ref, wb_ref, ends_ref, projected_ref, hot_ref)),
        )
        for turn in range(hot_ref.shape[0])
    )


def backward_tile(
    codes_ref, packed_ref, projected_ref, entry_ref, w_ref, ends_ref, a_ref, wb_ref, wanted_ref,
    own_ref, upper_ref, hot_ref, ct_ref, ts_ref
):
    channels, length = projected_ref.shape
    steps = length // 8
    index = lax.broadcasted_iota(jnp.int32, (8, length), 0)
    hot_rows(wanted_ref, codes_ref[...].astype(jnp.int32).astype(F32), hot_ref)
    yield True
    packed = packed_ref[...].astype(jnp.int32).astype(F32)
    scale = jnp.exp2(packed[channels : channels + 1, :]) * (1.0 / FULL)
    pixel_grad = (projected_ref[...] - packed[0:channels] * scale).astype(BF16)
    padded = jnp.concatenate([pixel_grad, jnp.zeros((16, length), BF16)], axis=0)
    yield True
    for first in range(0, length, 64):
        ct_ref[first : first + 64, :] = dot(entry_ref[first : first + 64, :], padded, NN)
    yield True
    total = jnp.zeros((8, length), F32)
    for i in range(steps):
        rows = pl.ds(8 * i, 8)
        total = total + w_ref[rows, :] * ct_ref[rows, :]
    yield True
    start, factor = ends_ref[0:8, :], ends_ref[8:16, :]
    total = jnp.where(start > 0.0, total / start, 0.0)
    for by in (1, 2, 4):
        total = total + factor * shift_rows(total, -by, 0.0, index)
        factor = factor * shift_rows(factor, -by, 1.0, index)
    after = shift_rows(total, -1, 0.0, index)
    for i in reversed(range(steps)):
        rows = pl.ds(8 * i, 8)
        gap = ct_ref[rows, :] - after
        term = w_ref[rows, :] * gap
        after = after + a_ref[rows, :] * gap
        ts_ref[rows, :] = term[:, 0:128] + term[:, 128:256]
    yield True
    feature_grad = dot(pixel_grad, wb_ref[...], NT)
    yield True
    logit_row = jnp.broadcast_to(jnp.sum(ts_ref[...].T, axis=0, keepdims=True), (8, length))
    grad_hi = feature_grad.astype(BF16)
    grad_lo = (feature_grad - grad_hi.astype(F32)).astype(BF16)
    logit_hi = logit_row.astype(BF16).astype(F32)
    logit_both = jnp.concatenate([logit_hi, logit_row - logit_hi], axis=0).astype(BF16)
    values = jnp.concatenate([grad_hi, grad_lo, logit_both], axis=0)
    yield True
    spread = dot(values, hot_ref[...], NT)
    c = channels
    for ref, first in ((own_ref, 0), (upper_ref, length)):
        part = spread[:, first : first + length]
        ref[0:c, :] += part[0:c] + part[c : 2 * c]
        ref[c : c + 8, :] += part[2 * c : 2 * c + 8] + part[2 * c + 8 : 2 * c + 16]


def backward_kernel(*refs):
    count = (len(refs) - 7) // 2
    sources, (own_ref, upper_ref) = refs[:count], refs[count : count + 2]
    held = refs[count + 2 : 2 * count + 2]
    wanted_ref, hot_ref, ct_ref, ts_ref, sem = refs[2 * count + 2 :]
    group, turns = hot_ref.shape[0], sem.shape[0]

    def copies(turn):
        span = pl.ds(turn * group, group)
        return [
            pltpu.make_async_copy(source.at[span], place.at[span], sem.at[turn, index])
            for index, (source, place) in enumerate(zip(sources, held))
        ]

    for turn in range(turns):
        for copy in copies(turn):
            copy.start()
    set_wanted(wanted_ref)
    own_ref[...] = jnp.zeros(own_ref.shape, F32)
    upper_ref[...] = jnp.zeros(upper_ref.shape, F32)

    def build(turn, carry):
        pending = copies(turn)

        def arrived(first, last):
            def wait():
                for copy in pending[first:last]:
                    copy.wait()

            return wait

        in_turns(
            (
                backward_tile(
                    *(ref.at[turn * group + step] for ref in held),
                    wanted_ref, own_ref, upper_ref, hot_ref.at[step], ct_ref.at[step], ts_ref.at[step],
                )
                for step in range(group)
            ),
            (arrived(0, 1), arrived(1, 8)),
        )
        return carry

    lax.fori_loop(0, turns, build, 0)


def finish_kernel(own_ref, returned_ref, logits_ref, feature_ref, logit_ref):
    channels = feature_ref.shape[0]
    feature_ref[...] = own_ref[0:channels, :] + returned_ref[0:channels, :]
    summed = own_ref[channels : channels + 1, :] + returned_ref[channels : channels + 1, :]
    logit_ref[...] = summed / (1.0 + jnp.exp(logits_ref[...]))


def whole():
    return pl.BlockSpec(memory_space=pltpu.VMEM)


def small():
    return pltpu.CompilerParams(vmem_limit_bytes=8 << 20)


def blocks(group, *shape):
    return pl.BlockSpec((group,) + shape, lambda t: (t,) + (0,) * len(shape))


def fixed(*shape):
    return pl.BlockSpec(shape, lambda t: (0,) * len(shape))


def kept_sizes(channels, length):
    return (
        ((length, channels + 16), BF16),
        ((length, length), F32),
        ((length, length), F32),
        ((length, length), BF16),
        ((16, length), F32),
        ((channels, length), F32),
    )


def forward(codes, terms, feature_bf, decoder, group=4):
    channels, decoded = decoder.shape
    views, length = codes.shape[0], codes.shape[2]
    shape = jax.ShapeDtypeStruct
    kept = kept_sizes(channels, length)
    return pl.pallas_call(
        forward_kernel,
        out_shape=tuple(shape((views,) + size, kind) for size, kind in kept),
        grid=(views // group,),
        in_specs=[
            blocks(group, 8, length),
            blocks(group, 16, 2 * length),
            fixed(channels, 2 * length),
            fixed(channels, decoded),
        ],
        out_specs=tuple(blocks(group, *size) for size, _ in kept),
        scratch_shapes=[
            pltpu.VMEM((channels, 3 * channels), BF16),
            pltpu.VMEM((channels + 16, length), BF16),
            pltpu.VMEM((2 * length, 128), BF16),
            pltpu.VMEM((group, 2 * length, length), BF16),
        ],
        cost_estimate=pl.CostEstimate(
            flops=views * 2 * length * length * 600,
            bytes_accessed=views * length * length * 11,
            transcendentals=views * length * length,
        ),
        name="forward",
    )(codes, terms, feature_bf, decoder)


def backward(received, codes, saved, group=4):
    channels = saved[-1].shape[1]
    views, length = codes.shape[0], codes.shape[2]
    shape = jax.ShapeDtypeStruct
    entry, a, w, wb, ends, projected = saved
    operands = (codes, received, projected, entry, w, ends, a, wb)
    return pl.pallas_call(
        backward_kernel,
        out_shape=(shape((channels + 8, length), F32),) * 2,
        in_specs=[pl.BlockSpec(memory_space=pl.ANY)] * len(operands),
        out_specs=(whole(),) * 2,
        scratch_shapes=[
            *(pltpu.VMEM(operand.shape, operand.dtype) for operand in operands),
            pltpu.VMEM((2 * length, 128), BF16),
            pltpu.VMEM((group, 2 * length, length), BF16),
            pltpu.VMEM((group, length, length), F32),
            pltpu.VMEM((group, length, 128), F32),
            pltpu.SemaphoreType.DMA((views // group, len(operands))),
        ],
        cost_estimate=pl.CostEstimate(
            flops=views * 2 * length * length * 600,
            bytes_accessed=views * length * length * 11,
            transcendentals=0,
        ),
        name="backward",
    )(*operands)


def pack(decoder, targets, group=4):
    channels = decoder.shape[0]
    tiles, length, decoded = targets.shape
    shape = (tiles, channels + 8, length)
    return pl.pallas_call(
        pack_kernel,
        out_shape=jax.ShapeDtypeStruct(shape, jnp.int16),
        in_specs=[whole(), pl.BlockSpec(memory_space=pl.ANY)],
        out_specs=pl.BlockSpec(memory_space=pl.ANY),
        scratch_shapes=[
            pltpu.VMEM(targets.shape, BF16),
            pltpu.VMEM(shape, jnp.int16),
            pltpu.SemaphoreType.DMA((tiles,)),
            pltpu.SemaphoreType.DMA((tiles // group,)),
        ],
        cost_estimate=pl.CostEstimate(
            flops=2 * tiles * length * channels * decoded,
            bytes_accessed=tiles * length * (2 * decoded + 2 * channels),
            transcendentals=0,
        ),
        name="pack",
    )(decoder, targets)


def on_device(features, positions, spreads, logits, camera, decoder, tile_lists, counts, targets):
    channels, length = features.shape
    tiles = tile_lists.shape[2]
    views = camera.shape[0]
    column = lax.axis_index("cam")
    tile_row = lax.axis_index("space")
    image_width = TS * lax.axis_size("cam")
    image_height = TS * lax.axis_size("space")
    shape = jax.ShapeDtypeStruct

    coded = pl.pallas_call(
        list_kernel,
        out_shape=shape((tiles, 8, length), jnp.int16),
        in_specs=[whole(), pl.BlockSpec(memory_space=pltpu.SMEM)],
        out_specs=whole(),
        compiler_params=small(),
        cost_estimate=pl.CostEstimate(flops=1000000, bytes_accessed=100000, transcendentals=0),
        name="lists",
    )(tile_lists[0, 0], counts[0, 0])
    codes = lax.all_to_all(coded, "cam", 0, 0, tiled=True)
    own_slab = jnp.concatenate([features, positions, spreads[None], logits[None]], axis=0)
    upper_slab = shifted(own_slab, "space", 1)

    packed = pack(decoder, targets[0, 0])
    packed, upper_slab = lax.optimization_barrier((packed, upper_slab))
    received = lax.all_to_all(packed, "cam", 0, 0, tiled=True)

    place = jnp.stack(
        [
            0.5 * image_width - (column * TS + 0.5 * TS),
            0.5 * image_height - (tile_row * TS + 0.5 * TS),
            tile_row,
        ]
    ).astype(F32)
    feature_bf, terms = pl.pallas_call(
        prep_kernel,
        out_shape=(shape((channels, 2 * length), BF16), shape((views, 16, 2 * length), BF16)),
        in_specs=[
            pl.BlockSpec(memory_space=pltpu.SMEM),
            pl.BlockSpec(memory_space=pltpu.SMEM),
            whole(),
            whole(),
        ],
        out_specs=(whole(), whole()),
        scratch_shapes=[pltpu.VMEM((16, 2 * length), F32)],
        cost_estimate=pl.CostEstimate(flops=10000000, bytes_accessed=1000000, transcendentals=20000),
        name="prep",
    )(camera, place, own_slab, upper_slab)

    saved = forward(codes, terms, feature_bf, decoder)
    own_sum, upper_sum = backward(received, codes, saved)
    returned = shifted(upper_sum, "space", -1)
    grad_features, grad_logits = pl.pallas_call(
        finish_kernel,
        out_shape=(shape((channels, length), F32), shape((1, length), F32)),
        in_specs=[whole(), whole(), whole()],
        out_specs=(whole(), whole()),
        compiler_params=small(),
        name="finish",
    )(own_sum, returned, logits[None])
    return grad_features, grad_logits[0]


def solution(mesh):
    placed = (
        P(None, ("cam", "space")),
        P(None, ("cam", "space")),
        P(("cam", "space")),
        P(("cam", "space")),
        P(),
        P(),
        P("cam", "space", None, None),
        P("cam", "space", None),
        P("cam", "space", None, None, None),
    )
    return jax.shard_map(
        on_device,
        mesh=mesh,
        in_specs=placed,
        out_specs=(P(None, ("cam", "space")), P(("cam", "space"))),
        check_vma=False,
    )
```

```python
import jax
import jax.numpy as jnp
from jax import lax
from jax.experimental import pallas as pl
from jax.experimental.pallas import tpu as pltpu
from jax.sharding import PartitionSpec as P

TS = 16
F32 = jnp.float32
BF16 = jnp.bfloat16
DEAD = 512.0
FULL = 32000.0
NN = (((1,), (0,)), ((), ()))
NT = (((1,), (1,)), ((), ()))
LOG2E = 1.4426950408889634


def dot(left, right, dims):
    return lax.dot_general(left, right, dims, preferred_element_type=F32)


def shifted(shard, axis, by):
    length = lax.axis_size(axis)
    pairs = [(i, i + by) for i in range(length) if 0 <= i + by < length]
    return lax.ppermute(shard, axis, pairs)


def pieces(value):
    first = value.astype(BF16).astype(F32)
    rest = value - first
    second = rest.astype(BF16).astype(F32)
    third = (rest - second).astype(BF16).astype(F32)
    return first, second, third


def list_kernel(ids_ref, counts_ref, out_ref):
    tiles, length = ids_ref.shape
    segment = length // 8
    ids = ids_ref[...]
    row = lax.broadcasted_iota(jnp.int32, (tiles, length), 0)
    entry = lax.broadcasted_iota(jnp.int32, (tiles, length), 1)
    above = ids >= tiles * length
    inside = jnp.where(above, ids - tiles * length, ids) - row * length
    code = jnp.where(above, -1 - inside, inside).astype(F32)
    live = jnp.zeros((tiles, length), jnp.int32)
    for tile in range(tiles):
        live = jnp.where(row == tile, counts_ref[tile], live)
    code = jnp.where(entry < live, code, DEAD)
    source = lax.broadcasted_iota(jnp.int32, (length, length), 0)
    place = lax.broadcasted_iota(jnp.int32, (length, length), 1)
    chosen = source == segment * (place % 8) + place // 8
    codes = dot(code.astype(BF16), chosen.astype(F32).astype(BF16), NN).astype(jnp.int32)
    for tile in range(tiles):
        out_ref[tile] = jnp.broadcast_to(codes[tile : tile + 1, :], (8, length)).astype(jnp.int16)


def pack_kernel(decoder_ref, targets_ref, out_ref, held_ref, built_ref, in_sem, out_sem):
    channels = decoder_ref.shape[0]
    tiles = held_ref.shape[0]
    group = tiles // out_sem.shape[0]

    def incoming(tile):
        return pltpu.make_async_copy(targets_ref.at[tile], held_ref.at[tile], in_sem.at[tile])

    def outgoing(turn):
        span = pl.ds(turn * group, group)
        return pltpu.make_async_copy(built_ref.at[span], out_ref.at[span], out_sem.at[turn])

    for tile in range(tiles):
        incoming(tile).start()

    def build(turn, carry):
        for step in range(group):
            incoming(turn * group + step).wait()
        for step in range(group):
            tile = turn * group + step
            value = dot(held_ref[tile], decoder_ref[...], NT).T
            largest = jnp.max(jnp.abs(value), axis=0, keepdims=True)
            power = jnp.floor(jnp.log2(jnp.maximum(largest, 1e-30))) + 1.0
            fixed_point = jnp.round(value * (FULL * jnp.exp2(-power)))
            built_ref[tile, 0:channels, :] = fixed_point.astype(jnp.int32).astype(jnp.int16)
            powers = jnp.broadcast_to(power, (8, value.shape[1]))
            built_ref[tile, channels : channels + 8, :] = powers.astype(jnp.int32).astype(jnp.int16)
        outgoing(turn).start()
        return carry

    lax.fori_loop(0, out_sem.shape[0], build, 0)
    for turn in range(out_sem.shape[0]):
        outgoing(turn).wait()


def prep_kernel(camera_ref, own_ref, upper_ref, feature_ref, terms_ref, row_ref):
    channels, length = feature_ref.shape[0], own_ref.shape[1]
    views, lines = terms_ref.shape[0], terms_ref.shape[1]
    column = lax.axis_index("cam").astype(F32)
    tile_row = lax.axis_index("space")
    band = tile_row.astype(F32)
    feature_ref[:, 0:length] = own_ref[0:channels, :].astype(BF16)
    feature_ref[:, length:] = upper_ref[0:channels, :].astype(BF16)

    def both(row):
        own = own_ref[row : row + 1, :]
        upper = jnp.where(tile_row > 0, upper_ref[row : row + 1, :], own)
        return jnp.broadcast_to(jnp.concatenate([own, upper], axis=1), (views, 2 * length))

    def viewer(part):
        index = lax.broadcasted_iota(jnp.int32, (views, 128), 0)
        value = jnp.zeros((views, 128), F32)
        for view in range(views):
            value = jnp.where(index == view, camera_ref[part, view], value)
        return jnp.concatenate([value] * (2 * length // 128), axis=1)

    place_x, place_y, depth, spread, logit = (both(channels + i) for i in range(5))
    log_open = LOG2E * (
        jnp.log(0.99) - (jnp.maximum(-logit, 0.0) + jnp.log(1.0 + jnp.exp(-jnp.abs(logit))))
    )
    distance = depth - 0.05 * viewer(2)
    u = (place_x - 0.75 * TS * viewer(0)) / distance
    v = (place_y - 0.75 * TS * viewer(1)) / distance
    u = u + (0.5 * TS * lax.axis_size("cam") - (column * TS + 0.5 * TS))
    v = v + (0.5 * TS * lax.axis_size("space") - (band * TS + 0.5 * TS))
    radius = spread / distance
    inverse = (0.5 * LOG2E) / (radius * radius)
    terms = (log_open - inverse * (u * u + v * v), 2.0 * inverse * u, 2.0 * inverse * v, -inverse)
    values = [piece for term in terms for piece in pieces(term)]
    values += [jnp.zeros((views, 2 * length), F32)] * (lines - len(values))
    for block in range(2 * length // 128):
        lanes = slice(128 * block, 128 * (block + 1))
        for index, value in enumerate(values):
            row_ref[block, pl.ds(index, views, stride=lines), :] = value[:, lanes]
        for view in range(views):
            terms_ref[view, :, lanes] = row_ref[block, lines * view : lines * (view + 1), :].astype(BF16)


def shift_rows(value, by, fill, index):
    moved = pltpu.roll(value, by % 8, 0)
    inside = index >= by if by > 0 else index < 8 + by
    return jnp.where(inside, moved, fill)


def in_turns(works, before=()):
    works, stage = list(works), 0
    while works:
        if stage < len(before):
            before[stage]()
        works = [work for work in works if next(work, None) is not None]
        stage += 1


def hot_rows(wanted_ref, codes, hot_ref):
    code = jnp.concatenate([codes, codes], axis=0).astype(BF16)
    half = wanted_ref.shape[1]
    one, zero = jnp.ones((16, half), BF16), jnp.zeros((16, half), BF16)
    for first in range(0, hot_ref.shape[0], 16):
        wanted = wanted_ref[first : first + 16, :]
        for side in range(0, code.shape[1], half):
            hot_ref[first : first + 16, side : side + half] = jnp.where(
                wanted == code[:, side : side + half], one, zero
            )


def set_wanted(wanted_ref):
    slot = lax.broadcasted_iota(jnp.int32, wanted_ref.shape, 0)
    length = wanted_ref.shape[0] // 2
    wanted_ref[...] = jnp.where(slot < length, slot, length - 1 - slot).astype(F32).astype(BF16)


def forward_tile(
    codes_ref, terms_ref, feature_ref, squares_ref, basis_ref, wanted_ref,
    entry_ref, a_ref, w_ref, wb_ref, ends_ref, projected_ref, hot_ref
):
    channels = feature_ref.shape[0]
    length = codes_ref.shape[1]
    steps = length // 8
    codes = codes_ref[...].astype(jnp.int32).astype(F32)
    hot_rows(wanted_ref, codes, hot_ref)
    yield True
    table = jnp.concatenate([feature_ref[...], terms_ref[...]], axis=0)
    picked = dot(table, hot_ref[...], NN)
    feature_t = picked[0:channels].astype(BF16)
    line = lax.broadcasted_iota(jnp.int32, (16, length), 0)
    dead = jnp.where(codes[0:1, :] == DEAD, -32768.0, 0.0)
    lower = jnp.where(line == 12, dead, picked[channels:])
    entry_ref[...] = jnp.concatenate([picked[0:channels], lower], axis=0).T.astype(BF16)
    yield True
    for first in range(0, length, 64):
        a_ref[first : first + 64, :] = jnp.exp2(dot(entry_ref[first : first + 64, :], basis_ref[...], NN))
    yield True
    index = lax.broadcasted_iota(jnp.int32, (8, length), 0)
    keep = jnp.ones((8, length), F32)
    for i in range(steps):
        rows = pl.ds(8 * i, 8)
        local = a_ref[rows, :] * keep
        w_ref[rows, :] = local
        keep = keep - local
    start = shift_rows(keep, 1, 1.0, index)
    for by in (1, 2, 4):
        start = start * shift_rows(start, by, 1.0, index)
    ends_ref[0:8, :] = start
    ends_ref[8:16, :] = keep
    yield True
    both = jnp.concatenate([start, start], axis=0)
    for i in range(steps // 2):
        rows = pl.ds(16 * i, 16)
        weight = w_ref[rows, :] * both
        w_ref[rows, :] = weight
        wb_ref[rows, :] = weight.astype(BF16)
    yield True
    composite = dot(feature_t, wb_ref[...], NN).astype(BF16)
    projected_ref[...] = dot(squares_ref[...], jnp.concatenate([composite] * 3, axis=0), NN)


def forward_kernel(
    codes_ref, terms_ref, feature_ref, decoder_ref,
    entry_ref, a_ref, w_ref, wb_ref, ends_ref, projected_ref,
    squares_ref, basis_ref, wanted_ref, hot_ref
):
    channels = feature_ref.shape[0]

    @pl.when(pl.program_id(0) == 0)
    def _():
        set_wanted(wanted_ref)
        for turn, piece in enumerate(pieces(dot(decoder_ref[...], decoder_ref[...], NT))):
            squares_ref[:, channels * turn : channels * (turn + 1)] = piece.astype(BF16)
        line = lax.broadcasted_iota(jnp.int32, basis_ref.shape, 0) - channels
        pixel = lax.broadcasted_iota(jnp.int32, basis_ref.shape, 1)
        px = (pixel % TS).astype(F32) - (0.5 * TS - 0.5)
        py = (pixel // TS).astype(F32) - (0.5 * TS - 0.5)
        basis = jnp.where(line < 3, 1.0, jnp.where(line < 6, px, jnp.where(line < 9, py, px * px + py * py)))
        basis = jnp.where(line == 12, 1.0, basis)
        basis_ref[...] = jnp.where((line < 0) | (line > 12), 0.0, basis).astype(BF16)

    in_turns(
        forward_tile(
            codes_ref.at[turn], terms_ref.at[turn],
            feature_ref, squares_ref, basis_ref, wanted_ref,
            *(ref.at[turn] for ref in (entry_ref, a_ref, w_ref, wb_ref, ends_ref, projected_ref, hot_ref)),
        )
        for turn in range(hot_ref.shape[0])
    )


def backward_tile(
    codes_ref, packed_ref, projected_ref, entry_ref, w_ref, ends_ref, a_ref, wb_ref, wanted_ref,
    own_ref, upper_ref, hot_ref, ct_ref, ts_ref
):
    channels, length = projected_ref.shape
    steps = length // 8
    index = lax.broadcasted_iota(jnp.int32, (8, length), 0)
    hot_rows(wanted_ref, codes_ref[...].astype(jnp.int32).astype(F32), hot_ref)
    yield True
    packed = packed_ref[...].astype(jnp.int32).astype(F32)
    scale = jnp.exp2(packed[channels : channels + 1, :]) * (1.0 / FULL)
    pixel_grad = (projected_ref[...] - packed[0:channels] * scale).astype(BF16)
    padded = jnp.concatenate([pixel_grad, jnp.zeros((16, length), BF16)], axis=0)
    yield True
    for first in range(0, length, 64):
        ct_ref[first : first + 64, :] = dot(entry_ref[first : first + 64, :], padded, NN)
    yield True
    total = jnp.zeros((8, length), F32)
    for i in range(steps):
        rows = pl.ds(8 * i, 8)
        total = total + w_ref[rows, :] * ct_ref[rows, :]
    yield True
    start, factor = ends_ref[0:8, :], ends_ref[8:16, :]
    total = jnp.where(start > 0.0, total / start, 0.0)
    for by in (1, 2, 4):
        total = total + factor * shift_rows(total, -by, 0.0, index)
        factor = factor * shift_rows(factor, -by, 1.0, index)
    after = shift_rows(total, -1, 0.0, index)
    for i in reversed(range(steps)):
        rows = pl.ds(8 * i, 8)
        gap = ct_ref[rows, :] - after
        term = w_ref[rows, :] * gap
        after = after + a_ref[rows, :] * gap
        ts_ref[rows, :] = term[:, 0:128] + term[:, 128:256]
    yield True
    feature_grad = dot(pixel_grad, wb_ref[...], NT)
    yield True
    logit_row = jnp.broadcast_to(jnp.sum(ts_ref[...].T, axis=0, keepdims=True), (8, length))
    grad_hi = feature_grad.astype(BF16)
    grad_lo = (feature_grad - grad_hi.astype(F32)).astype(BF16)
    logit_hi = logit_row.astype(BF16).astype(F32)
    logit_both = jnp.concatenate([logit_hi, logit_row - logit_hi], axis=0).astype(BF16)
    values = jnp.concatenate([grad_hi, grad_lo, logit_both], axis=0)
    yield True
    spread = dot(values, hot_ref[...], NT)
    c = channels
    for ref, first in ((own_ref, 0), (upper_ref, length)):
        part = spread[:, first : first + length]
        ref[0:c, :] += part[0:c] + part[c : 2 * c]
        ref[c : c + 8, :] += part[2 * c : 2 * c + 8] + part[2 * c + 8 : 2 * c + 16]


def backward_kernel(*refs):
    count = (len(refs) - 7) // 2
    sources, (own_ref, upper_ref) = refs[:count], refs[count : count + 2]
    held = refs[count + 2 : 2 * count + 2]
    wanted_ref, hot_ref, ct_ref, ts_ref, sem = refs[2 * count + 2 :]
    group, turns = hot_ref.shape[0], sem.shape[0]

    def copies(turn):
        span = pl.ds(turn * group, group)
        return [
            pltpu.make_async_copy(source.at[span], place.at[span], sem.at[turn, index])
            for index, (source, place) in enumerate(zip(sources, held))
        ]

    for turn in range(turns):
        for copy in copies(turn):
            copy.start()
    set_wanted(wanted_ref)
    own_ref[...] = jnp.zeros(own_ref.shape, F32)
    upper_ref[...] = jnp.zeros(upper_ref.shape, F32)

    def build(turn, carry):
        pending = copies(turn)

        def arrived(first, last):
            def wait():
                for copy in pending[first:last]:
                    copy.wait()

            return wait

        in_turns(
            (
                backward_tile(
                    *(ref.at[turn * group + step] for ref in held),
                    wanted_ref, own_ref, upper_ref, hot_ref.at[step], ct_ref.at[step], ts_ref.at[step],
                )
                for step in range(group)
            ),
            (arrived(0, 1), arrived(1, 8)),
        )
        return carry

    lax.fori_loop(0, turns, build, 0)


def finish_kernel(own_ref, returned_ref, logits_ref, feature_ref, logit_ref):
    channels = feature_ref.shape[0]
    feature_ref[...] = own_ref[0:channels, :] + returned_ref[0:channels, :]
    summed = own_ref[channels : channels + 1, :] + returned_ref[channels : channels + 1, :]
    logit_ref[...] = summed / (1.0 + jnp.exp(logits_ref[...]))


def whole():
    return pl.BlockSpec(memory_space=pltpu.VMEM)


def small():
    return pltpu.CompilerParams(vmem_limit_bytes=8 << 20)


def blocks(group, *shape):
    return pl.BlockSpec((group,) + shape, lambda t: (t,) + (0,) * len(shape))


def fixed(*shape):
    return pl.BlockSpec(shape, lambda t: (0,) * len(shape))


def kept_sizes(channels, length):
    return (
        ((length, channels + 16), BF16),
        ((length, length), F32),
        ((length, length), F32),
        ((length, length), BF16),
        ((16, length), F32),
        ((channels, length), F32),
    )


def forward(codes, terms, feature_bf, decoder, group=4):
    channels, decoded = decoder.shape
    views, length = codes.shape[0], codes.shape[2]
    shape = jax.ShapeDtypeStruct
    kept = kept_sizes(channels, length)
    return pl.pallas_call(
        forward_kernel,
        out_shape=tuple(shape((views,) + size, kind) for size, kind in kept),
        grid=(views // group,),
        in_specs=[
            blocks(group, 8, length),
            blocks(group, 16, 2 * length),
            fixed(channels, 2 * length),
            fixed(channels, decoded),
        ],
        out_specs=tuple(blocks(group, *size) for size, _ in kept),
        scratch_shapes=[
            pltpu.VMEM((channels, 3 * channels), BF16),
            pltpu.VMEM((channels + 16, length), BF16),
            pltpu.VMEM((2 * length, 128), BF16),
            pltpu.VMEM((group, 2 * length, length), BF16),
        ],
        cost_estimate=pl.CostEstimate(
            flops=views * 2 * length * length * 600,
            bytes_accessed=views * length * length * 11,
            transcendentals=views * length * length,
        ),
        name="forward",
    )(codes, terms, feature_bf, decoder)


def backward(received, codes, saved, group=4):
    channels = saved[-1].shape[1]
    views, length = codes.shape[0], codes.shape[2]
    shape = jax.ShapeDtypeStruct
    entry, a, w, wb, ends, projected = saved
    operands = (codes, received, projected, entry, w, ends, a, wb)
    return pl.pallas_call(
        backward_kernel,
        out_shape=(shape((channels + 8, length), F32),) * 2,
        in_specs=[pl.BlockSpec(memory_space=pl.ANY)] * len(operands),
        out_specs=(whole(),) * 2,
        scratch_shapes=[
            *(pltpu.VMEM(operand.shape, operand.dtype) for operand in operands),
            pltpu.VMEM((2 * length, 128), BF16),
            pltpu.VMEM((group, 2 * length, length), BF16),
            pltpu.VMEM((group, length, length), F32),
            pltpu.VMEM((group, length, 128), F32),
            pltpu.SemaphoreType.DMA((views // group, len(operands))),
        ],
        cost_estimate=pl.CostEstimate(
            flops=views * 2 * length * length * 600,
            bytes_accessed=views * length * length * 11,
            transcendentals=0,
        ),
        name="backward",
    )(*operands)


def pack(decoder, targets, group=4):
    channels = decoder.shape[0]
    tiles, length, decoded = targets.shape
    shape = (tiles, channels + 8, length)
    return pl.pallas_call(
        pack_kernel,
        out_shape=jax.ShapeDtypeStruct(shape, jnp.int16),
        in_specs=[whole(), pl.BlockSpec(memory_space=pl.ANY)],
        out_specs=pl.BlockSpec(memory_space=pl.ANY),
        scratch_shapes=[
            pltpu.VMEM(targets.shape, BF16),
            pltpu.VMEM(shape, jnp.int16),
            pltpu.SemaphoreType.DMA((tiles,)),
            pltpu.SemaphoreType.DMA((tiles // group,)),
        ],
        cost_estimate=pl.CostEstimate(
            flops=2 * tiles * length * channels * decoded,
            bytes_accessed=tiles * length * (2 * decoded + 2 * channels),
            transcendentals=0,
        ),
        name="pack",
    )(decoder, targets)


def on_device(features, positions, spreads, logits, camera, decoder, tile_lists, counts, targets):
    channels, length = features.shape
    tiles = tile_lists.shape[2]
    views = camera.shape[0]
    shape = jax.ShapeDtypeStruct

    coded = pl.pallas_call(
        list_kernel,
        out_shape=shape((tiles, 8, length), jnp.int16),
        in_specs=[whole(), pl.BlockSpec(memory_space=pltpu.SMEM)],
        out_specs=whole(),
        compiler_params=small(),
        cost_estimate=pl.CostEstimate(flops=1000000, bytes_accessed=100000, transcendentals=0),
        name="lists",
    )(tile_lists[0, 0], counts[0, 0])
    codes = lax.all_to_all(coded, "cam", 0, 0, tiled=True)
    own_slab = jnp.concatenate([features, positions, spreads[None], logits[None]], axis=0)
    upper_slab = shifted(own_slab, "space", 1)

    packed = pack(decoder, targets[0, 0])
    received = lax.all_to_all(packed, "cam", 0, 0, tiled=True)

    feature_bf, terms = pl.pallas_call(
        prep_kernel,
        out_shape=(shape((channels, 2 * length), BF16), shape((views, 16, 2 * length), BF16)),
        in_specs=[
            pl.BlockSpec(memory_space=pltpu.SMEM),
            whole(),
            whole(),
        ],
        out_specs=(whole(), whole()),
        scratch_shapes=[pltpu.VMEM((2 * length // 128, views * 16, 128), F32)],
        cost_estimate=pl.CostEstimate(flops=10000000, bytes_accessed=1000000, transcendentals=20000),
        name="prep",
    )(camera.T, own_slab, upper_slab)

    saved = forward(codes, terms, feature_bf, decoder)
    own_sum, upper_sum = backward(received, codes, saved)
    returned = shifted(upper_sum, "space", -1)
    grad_features, grad_logits = pl.pallas_call(
        finish_kernel,
        out_shape=(shape((channels, length), F32), shape((1, length), F32)),
        in_specs=[whole(), whole(), whole()],
        out_specs=(whole(), whole()),
        compiler_params=small(),
        name="finish",
    )(own_sum, returned, logits[None])
    return grad_features, grad_logits[0]


def solution(mesh):
    placed = (
        P(None, ("cam", "space")),
        P(None, ("cam", "space")),
        P(("cam", "space")),
        P(("cam", "space")),
        P(),
        P(),
        P("cam", "space", None, None),
        P("cam", "space", None),
        P("cam", "space", None, None, None),
    )
    return jax.shard_map(
        on_device,
        mesh=mesh,
        in_specs=placed,
        out_specs=(P(None, ("cam", "space")), P(("cam", "space"))),
        check_vma=False,
    )
```

```python
import jax
import jax.numpy as jnp
from jax import lax
from jax.experimental import pallas as pl
from jax.experimental.pallas import tpu as pltpu
from jax.sharding import PartitionSpec as P

TS = 16
F32 = jnp.float32
BF16 = jnp.bfloat16
DEAD = 512.0
FULL = 32000.0
NN = (((1,), (0,)), ((), ()))
NT = (((1,), (1,)), ((), ()))
LOG2E = 1.4426950408889634


def dot(left, right, dims):
    return lax.dot_general(left, right, dims, preferred_element_type=F32)


def shifted(shard, axis, by):
    length = lax.axis_size(axis)
    pairs = [(i, i + by) for i in range(length) if 0 <= i + by < length]
    return lax.ppermute(shard, axis, pairs)


def pieces(value):
    first = value.astype(BF16).astype(F32)
    rest = value - first
    second = rest.astype(BF16).astype(F32)
    third = (rest - second).astype(BF16).astype(F32)
    return first, second, third


def list_kernel(ids_ref, counts_ref, out_ref):
    tiles, length = ids_ref.shape
    segment = length // 8
    ids = ids_ref[...]
    row = lax.broadcasted_iota(jnp.int32, (tiles, length), 0)
    entry = lax.broadcasted_iota(jnp.int32, (tiles, length), 1)
    above = ids >= tiles * length
    inside = jnp.where(above, ids - tiles * length, ids) - row * length
    code = jnp.where(above, -1 - inside, inside).astype(F32)
    live = jnp.zeros((tiles, length), jnp.int32)
    for tile in range(tiles):
        live = jnp.where(row == tile, counts_ref[tile], live)
    code = jnp.where(entry < live, code, DEAD)
    source = lax.broadcasted_iota(jnp.int32, (length, length), 0)
    place = lax.broadcasted_iota(jnp.int32, (length, length), 1)
    chosen = source == segment * (place % 8) + place // 8
    codes = dot(code.astype(BF16), chosen.astype(F32).astype(BF16), NN).astype(jnp.int32)
    for tile in range(tiles):
        out_ref[tile] = jnp.broadcast_to(codes[tile : tile + 1, :], (8, length)).astype(jnp.int16)


def pack_kernel(decoder_ref, targets_ref, out_ref, held_ref, built_ref, in_sem, out_sem):
    channels = decoder_ref.shape[0]
    tiles = held_ref.shape[0]
    group = tiles // out_sem.shape[0]

    def incoming(tile):
        return pltpu.make_async_copy(targets_ref.at[tile], held_ref.at[tile], in_sem.at[tile])

    def outgoing(turn):
        span = pl.ds(turn * group, group)
        return pltpu.make_async_copy(built_ref.at[span], out_ref.at[span], out_sem.at[turn])

    for tile in range(tiles):
        incoming(tile).start()

    def build(turn, carry):
        for step in range(group):
            incoming(turn * group + step).wait()
        for step in range(group):
            tile = turn * group + step
            value = dot(held_ref[tile], decoder_ref[...], NT).T
            largest = jnp.max(jnp.abs(value), axis=0, keepdims=True)
            power = jnp.floor(jnp.log2(jnp.maximum(largest, 1e-30))) + 1.0
            fixed_point = jnp.round(value * (FULL * jnp.exp2(-power)))
            built_ref[tile, 0:channels, :] = fixed_point.astype(jnp.int32).astype(jnp.int16)
            powers = jnp.broadcast_to(power, (8, value.shape[1]))
            built_ref[tile, channels : channels + 8, :] = powers.astype(jnp.int32).astype(jnp.int16)
        outgoing(turn).start()
        return carry

    lax.fori_loop(0, out_sem.shape[0], build, 0)
    for turn in range(out_sem.shape[0]):
        outgoing(turn).wait()


def project(camera_ref, own_ref, upper_ref, feature_ref, terms_ref, row_ref):
    channels, length = feature_ref.shape[0], own_ref.shape[1]
    views, lines = terms_ref.shape[0], terms_ref.shape[1]
    column = lax.axis_index("cam").astype(F32)
    tile_row = lax.axis_index("space")
    band = tile_row.astype(F32)
    feature_ref[:, 0:length] = own_ref[0:channels, :].astype(BF16)
    feature_ref[:, length:] = upper_ref[0:channels, :].astype(BF16)

    def both(row):
        own = own_ref[row : row + 1, :]
        upper = jnp.where(tile_row > 0, upper_ref[row : row + 1, :], own)
        return jnp.broadcast_to(jnp.concatenate([own, upper], axis=1), (views, 2 * length))

    def viewer(part):
        index = lax.broadcasted_iota(jnp.int32, (views, 128), 0)
        value = jnp.zeros((views, 128), F32)
        for view in range(views):
            value = jnp.where(index == view, camera_ref[part, view], value)
        return jnp.concatenate([value] * (2 * length // 128), axis=1)

    place_x, place_y, depth, spread, logit = (both(channels + i) for i in range(5))
    log_open = LOG2E * (
        jnp.log(0.99) - (jnp.maximum(-logit, 0.0) + jnp.log(1.0 + jnp.exp(-jnp.abs(logit))))
    )
    distance = depth - 0.05 * viewer(2)
    u = (place_x - 0.75 * TS * viewer(0)) / distance
    v = (place_y - 0.75 * TS * viewer(1)) / distance
    u = u + (0.5 * TS * lax.axis_size("cam") - (column * TS + 0.5 * TS))
    v = v + (0.5 * TS * lax.axis_size("space") - (band * TS + 0.5 * TS))
    radius = spread / distance
    inverse = (0.5 * LOG2E) / (radius * radius)
    terms = (log_open - inverse * (u * u + v * v), 2.0 * inverse * u, 2.0 * inverse * v, -inverse)
    values = [piece for term in terms for piece in pieces(term)]
    values += [jnp.zeros((views, 2 * length), F32)] * (lines - len(values))
    for block in range(2 * length // 128):
        lanes = slice(128 * block, 128 * (block + 1))
        for index, value in enumerate(values):
            row_ref[block, pl.ds(index, views, stride=lines), :] = value[:, lanes]
        for view in range(views):
            terms_ref[view, :, lanes] = row_ref[block, lines * view : lines * (view + 1), :].astype(BF16)


def shift_rows(value, by, fill, index):
    moved = pltpu.roll(value, by % 8, 0)
    inside = index >= by if by > 0 else index < 8 + by
    return jnp.where(inside, moved, fill)


def in_turns(works, before=()):
    works, stage = list(works), 0
    while works:
        if stage < len(before):
            before[stage]()
        works = [work for work in works if next(work, None) is not None]
        stage += 1


def hot_rows(wanted_ref, codes, hot_ref):
    code = jnp.concatenate([codes, codes], axis=0).astype(BF16)
    half = wanted_ref.shape[1]
    one, zero = jnp.ones((16, half), BF16), jnp.zeros((16, half), BF16)
    for first in range(0, hot_ref.shape[0], 16):
        wanted = wanted_ref[first : first + 16, :]
        for side in range(0, code.shape[1], half):
            hot_ref[first : first + 16, side : side + half] = jnp.where(
                wanted == code[:, side : side + half], one, zero
            )


def set_wanted(wanted_ref):
    slot = lax.broadcasted_iota(jnp.int32, wanted_ref.shape, 0)
    length = wanted_ref.shape[0] // 2
    wanted_ref[...] = jnp.where(slot < length, slot, length - 1 - slot).astype(F32).astype(BF16)


def forward_tile(
    codes_ref, terms_ref, feature_ref, squares_ref, basis_ref, wanted_ref,
    entry_ref, a_ref, w_ref, wb_ref, ends_ref, projected_ref, hot_ref
):
    channels = feature_ref.shape[0]
    length = codes_ref.shape[1]
    steps = length // 8
    codes = codes_ref[...].astype(jnp.int32).astype(F32)
    hot_rows(wanted_ref, codes, hot_ref)
    yield True
    table = jnp.concatenate([feature_ref[...], terms_ref[...]], axis=0)
    picked = dot(table, hot_ref[...], NN)
    feature_t = picked[0:channels].astype(BF16)
    line = lax.broadcasted_iota(jnp.int32, (16, length), 0)
    dead = jnp.where(codes[0:1, :] == DEAD, -32768.0, 0.0)
    lower = jnp.where(line == 12, dead, picked[channels:])
    entry_ref[...] = jnp.concatenate([picked[0:channels], lower], axis=0).T.astype(BF16)
    yield True
    for first in range(0, length, 64):
        a_ref[first : first + 64, :] = jnp.exp2(dot(entry_ref[first : first + 64, :], basis_ref[...], NN))
    yield True
    index = lax.broadcasted_iota(jnp.int32, (8, length), 0)
    keep = jnp.ones((8, length), F32)
    for i in range(steps):
        rows = pl.ds(8 * i, 8)
        local = a_ref[rows, :] * keep
        w_ref[rows, :] = local
        keep = keep - local
    start = shift_rows(keep, 1, 1.0, index)
    for by in (1, 2, 4):
        start = start * shift_rows(start, by, 1.0, index)
    ends_ref[0:8, :] = start
    ends_ref[8:16, :] = keep
    yield True
    both = jnp.concatenate([start, start], axis=0)
    for i in range(steps // 2):
        rows = pl.ds(16 * i, 16)
        weight = w_ref[rows, :] * both
        w_ref[rows, :] = weight
        wb_ref[rows, :] = weight.astype(BF16)
    yield True
    composite = dot(feature_t, wb_ref[...], NN).astype(BF16)
    projected_ref[...] = dot(squares_ref[...], jnp.concatenate([composite] * 3, axis=0), NN)


def forward_kernel(codes_ref, camera_ref, block_ref, upper_ref, decoder_ref, *refs):
    count = (len(refs) - 8) // 2
    outs, held = refs[:count], refs[count : 2 * count]
    feature_ref, terms_ref, row_ref, squares_ref, basis_ref, wanted_ref, hot_ref, sem = refs[2 * count :]
    channels = feature_ref.shape[0]
    group, turns = hot_ref.shape[0], sem.shape[0]
    project(camera_ref, block_ref, upper_ref, feature_ref, terms_ref, row_ref)
    set_wanted(wanted_ref)
    for turn, piece in enumerate(pieces(dot(decoder_ref[...], decoder_ref[...], NT))):
        squares_ref[:, channels * turn : channels * (turn + 1)] = piece.astype(BF16)
    line = lax.broadcasted_iota(jnp.int32, basis_ref.shape, 0) - channels
    pixel = lax.broadcasted_iota(jnp.int32, basis_ref.shape, 1)
    px = (pixel % TS).astype(F32) - (0.5 * TS - 0.5)
    py = (pixel // TS).astype(F32) - (0.5 * TS - 0.5)
    basis = jnp.where(line < 3, 1.0, jnp.where(line < 6, px, jnp.where(line < 9, py, px * px + py * py)))
    basis = jnp.where(line == 12, 1.0, basis)
    basis_ref[...] = jnp.where((line < 0) | (line > 12), 0.0, basis).astype(BF16)

    def copies(turn, first, last):
        span = pl.ds(turn * group, group)
        return [
            pltpu.make_async_copy(held[index].at[span], outs[index].at[span], sem.at[turn, index])
            for index in range(first, last)
        ]

    def build(turn, carry):
        def leaving(first, last):
            def start():
                for copy in copies(turn, first, last):
                    copy.start()

            return start

        def nothing():
            pass

        tile = turn * group
        in_turns(
            (
                forward_tile(
                    codes_ref.at[tile + step], terms_ref.at[tile + step],
                    feature_ref, squares_ref, basis_ref, wanted_ref,
                    *(ref.at[tile + step] for ref in held), hot_ref.at[step],
                )
                for step in range(group)
            ),
            (nothing, nothing, nothing, leaving(0, 2), nothing, leaving(2, count - 1)),
        )
        leaving(count - 1, count)()
        return carry

    lax.fori_loop(0, turns, build, 0)
    for turn in range(turns):
        for copy in copies(turn, 0, count):
            copy.wait()


def backward_tile(
    codes_ref, packed_ref, projected_ref, entry_ref, w_ref, ends_ref, a_ref, wb_ref, wanted_ref,
    own_ref, upper_ref, hot_ref, ct_ref, ts_ref
):
    channels, length = projected_ref.shape
    steps = length // 8
    index = lax.broadcasted_iota(jnp.int32, (8, length), 0)
    hot_rows(wanted_ref, codes_ref[...].astype(jnp.int32).astype(F32), hot_ref)
    yield True
    packed = packed_ref[...].astype(jnp.int32).astype(F32)
    scale = jnp.exp2(packed[channels : channels + 1, :]) * (1.0 / FULL)
    pixel_grad = (projected_ref[...] - packed[0:channels] * scale).astype(BF16)
    padded = jnp.concatenate([pixel_grad, jnp.zeros((16, length), BF16)], axis=0)
    yield True
    for first in range(0, length, 64):
        ct_ref[first : first + 64, :] = dot(entry_ref[first : first + 64, :], padded, NN)
    yield True
    total = jnp.zeros((8, length), F32)
    for i in range(steps):
        rows = pl.ds(8 * i, 8)
        total = total + w_ref[rows, :] * ct_ref[rows, :]
    yield True
    start, factor = ends_ref[0:8, :], ends_ref[8:16, :]
    total = jnp.where(start > 0.0, total / start, 0.0)
    for by in (1, 2, 4):
        total = total + factor * shift_rows(total, -by, 0.0, index)
        factor = factor * shift_rows(factor, -by, 1.0, index)
    after = shift_rows(total, -1, 0.0, index)
    for i in reversed(range(steps)):
        rows = pl.ds(8 * i, 8)
        gap = ct_ref[rows, :] - after
        term = w_ref[rows, :] * gap
        after = after + a_ref[rows, :] * gap
        ts_ref[rows, :] = term[:, 0:128] + term[:, 128:256]
    yield True
    feature_grad = dot(pixel_grad, wb_ref[...], NT)
    yield True
    logit_row = jnp.broadcast_to(jnp.sum(ts_ref[...].T, axis=0, keepdims=True), (8, length))
    grad_hi = feature_grad.astype(BF16)
    grad_lo = (feature_grad - grad_hi.astype(F32)).astype(BF16)
    logit_hi = logit_row.astype(BF16).astype(F32)
    logit_both = jnp.concatenate([logit_hi, logit_row - logit_hi], axis=0).astype(BF16)
    values = jnp.concatenate([grad_hi, grad_lo, logit_both], axis=0)
    yield True
    spread = dot(values, hot_ref[...], NT)
    c = channels
    for ref, first in ((own_ref, 0), (upper_ref, length)):
        part = spread[:, first : first + length]
        ref[0:c, :] += part[0:c] + part[c : 2 * c]
        ref[c : c + 8, :] += part[2 * c : 2 * c + 8] + part[2 * c + 8 : 2 * c + 16]


def backward_kernel(*refs):
    count = (len(refs) - 7) // 2
    sources, (own_ref, upper_ref) = refs[:count], refs[count : count + 2]
    held = refs[count + 2 : 2 * count + 2]
    wanted_ref, hot_ref, ct_ref, ts_ref, sem = refs[2 * count + 2 :]
    group, turns = hot_ref.shape[0], sem.shape[0]

    def copies(turn):
        span = pl.ds(turn * group, group)
        return [
            pltpu.make_async_copy(source.at[span], place.at[span], sem.at[turn, index])
            for index, (source, place) in enumerate(zip(sources, held))
        ]

    for turn in range(turns):
        for copy in copies(turn):
            copy.start()
    set_wanted(wanted_ref)
    own_ref[...] = jnp.zeros(own_ref.shape, F32)
    upper_ref[...] = jnp.zeros(upper_ref.shape, F32)

    def build(turn, carry):
        pending = copies(turn)

        def arrived(first, last):
            def wait():
                for copy in pending[first:last]:
                    copy.wait()

            return wait

        in_turns(
            (
                backward_tile(
                    *(ref.at[turn * group + step] for ref in held),
                    wanted_ref, own_ref, upper_ref, hot_ref.at[step], ct_ref.at[step], ts_ref.at[step],
                )
                for step in range(group)
            ),
            (arrived(0, 1), arrived(1, 8)),
        )
        return carry

    lax.fori_loop(0, turns, build, 0)


def finish_kernel(own_ref, returned_ref, logits_ref, feature_ref, logit_ref):
    channels = feature_ref.shape[0]
    feature_ref[...] = own_ref[0:channels, :] + returned_ref[0:channels, :]
    summed = own_ref[channels : channels + 1, :] + returned_ref[channels : channels + 1, :]
    logit_ref[...] = summed / (1.0 + jnp.exp(logits_ref[...]))


def whole():
    return pl.BlockSpec(memory_space=pltpu.VMEM)


def small():
    return pltpu.CompilerParams(vmem_limit_bytes=8 << 20)


def kept_sizes(channels, length):
    return (
        ((length, channels + 16), BF16),
        ((length, length), F32),
        ((length, length), F32),
        ((length, length), BF16),
        ((16, length), F32),
        ((channels, length), F32),
    )


def forward(codes, camera_t, own_slab, upper_slab, decoder, group=4):
    channels, decoded = decoder.shape
    views, length = codes.shape[0], codes.shape[2]
    shape = jax.ShapeDtypeStruct
    kept = [shape((views,) + size, kind) for size, kind in kept_sizes(channels, length)]
    return pl.pallas_call(
        forward_kernel,
        out_shape=tuple(kept),
        in_specs=[whole(), pl.BlockSpec(memory_space=pltpu.SMEM), whole(), whole(), whole()],
        out_specs=(pl.BlockSpec(memory_space=pl.ANY),) * len(kept),
        scratch_shapes=[
            *(pltpu.VMEM(out.shape, out.dtype) for out in kept),
            pltpu.VMEM((channels, 2 * length), BF16),
            pltpu.VMEM((views, 16, 2 * length), BF16),
            pltpu.VMEM((2 * length // 128, views * 16, 128), F32),
            pltpu.VMEM((channels, 3 * channels), BF16),
            pltpu.VMEM((channels + 16, length), BF16),
            pltpu.VMEM((2 * length, 128), BF16),
            pltpu.VMEM((group, 2 * length, length), BF16),
            pltpu.SemaphoreType.DMA((views // group, len(kept))),
        ],
        cost_estimate=pl.CostEstimate(
            flops=views * 2 * length * length * 600,
            bytes_accessed=views * length * length * 11,
            transcendentals=views * length * length,
        ),
        name="forward",
    )(codes, camera_t, own_slab, upper_slab, decoder)


def backward(received, codes, saved, group=4):
    channels = saved[-1].shape[1]
    views, length = codes.shape[0], codes.shape[2]
    shape = jax.ShapeDtypeStruct
    entry, a, w, wb, ends, projected = saved
    operands = (codes, received, projected, entry, w, ends, a, wb)
    return pl.pallas_call(
        backward_kernel,
        out_shape=(shape((channels + 8, length), F32),) * 2,
        in_specs=[pl.BlockSpec(memory_space=pl.ANY)] * len(operands),
        out_specs=(whole(),) * 2,
        scratch_shapes=[
            *(pltpu.VMEM(operand.shape, operand.dtype) for operand in operands),
            pltpu.VMEM((2 * length, 128), BF16),
            pltpu.VMEM((group, 2 * length, length), BF16),
            pltpu.VMEM((group, length, length), F32),
            pltpu.VMEM((group, length, 128), F32),
            pltpu.SemaphoreType.DMA((views // group, len(operands))),
        ],
        cost_estimate=pl.CostEstimate(
            flops=views * 2 * length * length * 600,
            bytes_accessed=views * length * length * 11,
            transcendentals=0,
        ),
        name="backward",
    )(*operands)


def pack(decoder, targets, group=4):
    channels = decoder.shape[0]
    tiles, length, decoded = targets.shape
    shape = (tiles, channels + 8, length)
    return pl.pallas_call(
        pack_kernel,
        out_shape=jax.ShapeDtypeStruct(shape, jnp.int16),
        in_specs=[whole(), pl.BlockSpec(memory_space=pl.ANY)],
        out_specs=pl.BlockSpec(memory_space=pl.ANY),
        scratch_shapes=[
            pltpu.VMEM(targets.shape, BF16),
            pltpu.VMEM(shape, jnp.int16),
            pltpu.SemaphoreType.DMA((tiles,)),
            pltpu.SemaphoreType.DMA((tiles // group,)),
        ],
        cost_estimate=pl.CostEstimate(
            flops=2 * tiles * length * channels * decoded,
            bytes_accessed=tiles * length * (2 * decoded + 2 * channels),
            transcendentals=0,
        ),
        name="pack",
    )(decoder, targets)


def on_device(features, positions, spreads, logits, camera, decoder, tile_lists, counts, targets):
    channels, length = features.shape
    tiles = tile_lists.shape[2]
    shape = jax.ShapeDtypeStruct

    coded = pl.pallas_call(
        list_kernel,
        out_shape=shape((tiles, 8, length), jnp.int16),
        in_specs=[whole(), pl.BlockSpec(memory_space=pltpu.SMEM)],
        out_specs=whole(),
        cost_estimate=pl.CostEstimate(flops=1000000, bytes_accessed=100000, transcendentals=0),
        name="lists",
    )(tile_lists[0, 0], counts[0, 0])
    codes = lax.all_to_all(coded, "cam", 0, 0, tiled=True)
    own_slab = jnp.concatenate([features, positions, spreads[None], logits[None]], axis=0)
    upper_slab = shifted(own_slab, "space", 1)

    packed = pack(decoder, targets[0, 0])
    received = lax.all_to_all(packed, "cam", 0, 0, tiled=True)

    saved = forward(codes, camera.T, own_slab, upper_slab, decoder)
    own_sum, upper_sum = backward(received, codes, saved)
    returned = shifted(upper_sum, "space", -1)
    grad_features, grad_logits = pl.pallas_call(
        finish_kernel,
        out_shape=(shape((channels, length), F32), shape((1, length), F32)),
        in_specs=[whole(), whole(), whole()],
        out_specs=(whole(), whole()),
        compiler_params=small(),
        name="finish",
    )(own_sum, returned, logits[None])
    return grad_features, grad_logits[0]


def solution(mesh):
    placed = (
        P(None, ("cam", "space")),
        P(None, ("cam", "space")),
        P(("cam", "space")),
        P(("cam", "space")),
        P(),
        P(),
        P("cam", "space", None, None),
        P("cam", "space", None),
        P("cam", "space", None, None, None),
    )
    return jax.shard_map(
        on_device,
        mesh=mesh,
        in_specs=placed,
        out_specs=(P(None, ("cam", "space")), P(("cam", "space"))),
        check_vma=False,
    )
```
